32 devices in a mesh: grp: 4 (over x, core), seg: 4 (over z), mp: 2 (over y).
Axes of the slice: x: 2, y: 2, z: 4, core: 2. Of those that a mesh axis runs over, the one named last changes fastest.
Arguments:
- tokens: bfloat16 [4096, 4096], P(('grp', 'seg'), 'mp'), may hold values from -6 to 6
- x_weight: bfloat16 [4096, 4096], P(('grp', 'seg'), 'mp'), may hold values from -0.09375 to 0.09375
- y_weight: bfloat16 [4096, 4096], P(('grp', 'seg'), 'mp'), may hold values from -0.09375 to 0.09375
- out_weight: bfloat16 [4096, 4096], P('mp', ('grp', 'seg')), may hold values from -0.09375 to 0.09375
- conv_weight: float32 [4, 4096], P(None, 'mp'), may hold values from -3 to 3
- conv_bias: float32 [4096], P('mp'), may hold values from -3 to 3
- decay_gate: bfloat16 [16, 256, 256], P('mp'), may hold values from -0.375 to 0.375
- decay_bias: float32 [4096], P('mp'), may hold values from -4 to 4
- input_gate: bfloat16 [16, 256, 256], P('mp'), may hold values from -0.375 to 0.375
- input_bias: float32 [4096], P('mp'), may hold values from -4 to 4
- log_rate: float32 [4096], P('mp'), may hold values from -19 to -5, as said below
- phase: float32 [4096], P('mp'), may hold values from -3.140625 to 3.140625
Outputs:
- mixed: bfloat16 [4096, 4096], P(('grp', 'seg'), 'mp')
The draws below stay inside these ranges and needn't reach their ends.
Inputs may be any that keep to these rules, and one draw needn't show every extreme that they name: softplus(log_rate) lies between 1e-8 and 1e-2.
All inputs are finite; a program needn't handle non-finite values.
Results may differ from the reference program's by a relative error of at most 0.015.
Values may be sent and summed in bfloat16 or wider, within the bound.
No kernel may reach another device: no remote copies, remote signals or barrier semaphores. Data moves between devices by JAX's collectives and lax.ppermute only.
A program may use at most 128 MiB of HBM per device.

```python
import jax
import jax.numpy as jnp
from jax import lax

D = 4096
L = 4096
HEADS = 16
CONV = 4
HEAD_DIM = 256
TOKENS = 4096


def draw_log_rate(key, part):
    first_key = jax.random.fold_in(key, 11)
    rates = jnp.exp(jax.random.uniform(first_key, (L,), jnp.float32, jnp.log(1e-06), jnp.log(0.05)))
    return jnp.log(jnp.expm1(rates / 8.0)).astype(jnp.float32)


def level_of(own_key, extent, pieces, low, largest):
    level = 1.0
    for axis_at, blocks in pieces:
        draws = jax.random.uniform(jax.random.fold_in(jax.random.fold_in(own_key, 6), axis_at), (blocks,), jnp.float32, low / len(pieces), largest / len(pieces))
        level = level * jnp.repeat(jnp.exp(draws), extent[axis_at] // blocks).reshape((-1,) + (1,) * (len(extent) - 1 - axis_at))
    return level


def gaussian(stream_key, extent, deviation, most, cuts=(), kind=jnp.bfloat16):
    gain = level_of(stream_key, extent, cuts, -0.22, 0.18) if cuts else 1.0
    result = jax.random.normal(stream_key, extent, jnp.float32) * deviation * gain
    return jnp.minimum(jnp.maximum(result, -most), most).astype(kind)


def setup_inputs(seed: int = 0) -> dict:
    splits = jax.random.split(jax.random.key(seed), 13)
    return {
        "tokens": gaussian(splits[0], (TOKENS, D), 1.0, 6.0, ((0, 16), (1, 2))),
        "x_weight": gaussian(splits[1], (D, L), D ** -0.5, 0.09375, ((0, 16), (1, 2))),
        "y_weight": gaussian(splits[2], (D, L), D ** -0.5, 0.09375, ((0, 16), (1, 2))),
        "out_weight": gaussian(splits[3], (L, D), L ** -0.5, 0.09375, ((0, 2), (1, 16))),
        "conv_weight": gaussian(splits[4], (CONV, L), 0.5, 3.0, ((1, 2),), jnp.float32),
        "conv_bias": gaussian(splits[5], (L,), 0.5, 3.0, ((0, 2),), jnp.float32),
        "decay_gate": gaussian(splits[6], (HEADS, HEAD_DIM, HEAD_DIM), HEAD_DIM ** -0.5, 0.375, ((0, 2),)),
        "decay_bias": gaussian(splits[7], (L,), 1.0, 4.0, ((0, 2),), jnp.float32),
        "input_gate": gaussian(splits[8], (HEADS, HEAD_DIM, HEAD_DIM), HEAD_DIM ** -0.5, 0.375, ((0, 2),)),
        "input_bias": gaussian(splits[9], (L,), 1.0, 4.0, ((0, 2),), jnp.float32),
        "log_rate": draw_log_rate(jax.random.fold_in(splits[12], 71), 0),
        "phase": jnp.clip(jax.random.uniform(splits[11], (L,), jnp.float32, -3.140625, 3.140625), -3.140625, 3.140625),
    }


def reference(tokens, x_weight, y_weight, out_weight, conv_weight, conv_bias, decay_gate, decay_bias, input_gate, input_bias, log_rate, phase):
    x_proj = jnp.dot(tokens, x_weight, preferred_element_type=jnp.float32).astype(jnp.bfloat16)
    branch = jax.nn.gelu(jnp.dot(tokens, y_weight, preferred_element_type=jnp.float32))
    padded = jnp.concatenate([jnp.zeros((CONV - 1, L), jnp.float32), x_proj.astype(jnp.float32)], axis=0)
    convolved = conv_bias + jnp.zeros((TOKENS, L), jnp.float32)
    for offset in range(CONV):
        convolved = convolved + conv_weight[offset] * padded[CONV - 1 - offset:CONV - 1 - offset + TOKENS]
    convolved = convolved.astype(jnp.bfloat16)
    head_view = convolved.astype(jnp.float32).reshape(TOKENS, HEADS, HEAD_DIM)
    rate_gate = jax.nn.sigmoid(jnp.einsum('nhd,hde->nhe', head_view, decay_gate.astype(jnp.float32)).reshape(TOKENS, L) + decay_bias)
    input_open = jax.nn.sigmoid(jnp.einsum('nhd,hde->nhe', head_view, input_gate.astype(jnp.float32)).reshape(TOKENS, L) + input_bias)
    log_decay = -8.0 * rate_gate * jax.nn.softplus(log_rate)
    decay = jnp.exp(log_decay)
    drive = jnp.sqrt(-jnp.expm1(2.0 * log_decay)) * input_open * convolved.astype(jnp.float32)
    cosine = jnp.cos(phase)
    sine = jnp.sin(phase)

    def advance(state, inputs):
        state_real, state_imag = state
        step_decay, step_drive = inputs
        new_real = step_decay * (cosine * state_real - sine * state_imag) + step_drive
        new_imag = step_decay * (sine * state_real + cosine * state_imag)
        return ((new_real, new_imag), new_real)
    start_state = (jnp.zeros((L,), jnp.float32), jnp.zeros((L,), jnp.float32))
    final_state, real_parts = lax.scan(advance, start_state, (decay, drive))
    gated = (branch * real_parts).astype(jnp.bfloat16)
    return jnp.dot(gated, out_weight, preferred_element_type=jnp.float32).astype(jnp.bfloat16)
```

```python
import jax
import jax.numpy as jnp
from jax import lax
from jax.experimental import pallas as pl
from jax.experimental.pallas import tpu as pltpu
from jax.sharding import PartitionSpec as P


VMEM = pl.BlockSpec(memory_space=pltpu.VMEM)
SMEM = pl.BlockSpec(memory_space=pltpu.SMEM)
GRANT = 56 * 1024 * 1024


def shifted(value, axis, by):
    peers = lax.axis_size(axis)
    pairs = [(i, i + by) for i in range(peers) if 0 <= i + by < peers]
    return lax.ppermute(value, axis, pairs)


def carried_in(value, axis, join, neutral):
    count, mine = (lax.axis_size(axis), lax.axis_index(axis))
    pieces = lax.all_gather(value, axis)
    total = jnp.full_like(value, 0) + jnp.asarray(neutral, value.dtype)

    def turn(position, total):
        longer = join(total, pieces[position])
        return jnp.where(position < mine, longer, total)

    return lax.fori_loop(0, count - 1, turn, total)


def combine(earlier, later):
    first_real = earlier[0] * later[0] - earlier[1] * later[1]
    first_imag = earlier[0] * later[1] + earlier[1] * later[0]
    state_real = later[0] * earlier[2] - later[1] * earlier[3] + later[2]
    state_imag = later[0] * earlier[3] + later[1] * earlier[2] + later[3]
    return jnp.stack([first_real, first_imag, state_real, state_imag])


def neutral(count):
    ones_row = jnp.ones((count,), jnp.float32)
    zeros_row = jnp.zeros((count,), jnp.float32)
    return jnp.stack([ones_row, zeros_row, zeros_row, zeros_row])


def general(
    tokens,
    x_weight,
    y_weight,
    out_weight,
    conv_weight,
    conv_bias,
    decay_gate,
    decay_bias,
    input_gate,
    input_bias,
    log_rate,
    phase,
):
    source = lax.all_gather(tokens, "mp", axis=1, tiled=True)
    tokens_here = source.shape[0]
    width = x_weight.shape[1]

    def add_rows(shard_piece):
        return jnp.dot(source, shard_piece, preferred_element_type=jnp.float32)

    x_sum = add_rows(lax.all_gather(x_weight, ("grp", "seg"), axis=0, tiled=True))
    y_sum = add_rows(lax.all_gather(y_weight, ("grp", "seg"), axis=0, tiled=True))
    x_proj = x_sum.astype(jnp.bfloat16)
    branch = jax.nn.gelu(y_sum)
    taps = conv_weight.shape[0]
    last_rows = x_proj[tokens_here - (taps - 1) :]
    before = shifted(last_rows, ("grp", "seg"), 1)
    padded = jnp.concatenate([before, x_proj], axis=0).astype(jnp.float32)
    convolved = conv_bias + jnp.zeros((tokens_here, width), jnp.float32)
    for offset in range(taps):
        convolved = (
            convolved
            + conv_weight[offset] * padded[taps - 1 - offset : taps - 1 - offset + tokens_here]
        )
    convolved = convolved.astype(jnp.bfloat16)
    heads_here = decay_gate.shape[0]
    block_size = decay_gate.shape[1]
    head_view = convolved.reshape(tokens_here, heads_here, block_size)
    rate_gate = jax.nn.sigmoid(
        jnp.einsum(
            "nhd,hde->nhe", head_view, decay_gate, preferred_element_type=jnp.float32
        ).reshape(tokens_here, width)
        + decay_bias
    )
    input_open = jax.nn.sigmoid(
        jnp.einsum(
            "nhd,hde->nhe", head_view, input_gate, preferred_element_type=jnp.float32
        ).reshape(tokens_here, width)
        + input_bias
    )
    log_decay = -8.0 * rate_gate * jax.nn.softplus(log_rate)
    decay = jnp.exp(log_decay)
    drive = jnp.sqrt(-jnp.expm1(2.0 * log_decay)) * input_open * convolved.astype(jnp.float32)
    elements = jnp.stack(
        [decay * jnp.cos(phase), decay * jnp.sin(phase), drive, jnp.zeros_like(drive)]
    )
    running = lax.associative_scan(combine, elements, axis=1)
    summary = running[:, tokens_here - 1]
    identity = neutral(width)
    carry_in = carried_in(summary, ("grp", "seg"), combine, identity)
    state_real = running[2] + running[0] * carry_in[2] - running[1] * carry_in[3]
    gated = (branch * state_real).astype(jnp.bfloat16)
    partial_value = jnp.dot(
        gated,
        lax.all_gather(out_weight, ("grp", "seg"), axis=1, tiled=True),
        preferred_element_type=jnp.float32,
    )
    reduced = lax.psum_scatter(
        partial_value.astype(jnp.bfloat16), "mp", scatter_dimension=1, tiled=True
    )
    return reduced


def swap(value, axis, bit):
    count = lax.axis_size(axis)
    return lax.ppermute(value, axis, [(i, i ^ bit) for i in range(count)])


def spread(first):
    own, other = first
    near = [own, swap(other, "seg", 1)]
    bit = 2
    while bit < lax.axis_size("seg"):
        near = near + [swap(piece, "seg", bit) for piece in near]
        bit = bit * 2
    return [near, [swap(piece, "grp", 2) for piece in near]]


def build_assemble(rows, wide, segs, dtype):
    block = wide // 2 // segs

    def kernel(place, *refs):
        pieces, whole = refs[:-1], refs[-1]
        c, z, turn = place[0], place[1], place[2]
        zl = lax.rem(z, 2)
        for index, piece in enumerate(pieces):
            e, f, h = index // 4, index // 2 % 2, index % 2
            row = pl.multiple_of((c ^ e) * (2 * rows) + (zl ^ f) * rows, rows)
            half = turn ^ h
            for b in range(segs):
                for d in range(2):
                    source = pl.multiple_of(((c ^ d) * segs + (z ^ b)) * block, block)
                    target = pl.multiple_of(half * wide + (b * 2 + d) * block, block)
                    whole[pl.ds(row, rows), pl.ds(target, block)] = piece[
                        :, pl.ds(source, block)
                    ]

    return pl.pallas_call(
        kernel,
        out_shape=jax.ShapeDtypeStruct((4 * rows, 2 * wide), dtype),
        in_specs=[SMEM] + [VMEM] * 8,
        out_specs=VMEM,
        compiler_params=pltpu.CompilerParams(vmem_limit_bytes=GRANT),
        cost_estimate=pl.CostEstimate(
            flops=0, bytes_accessed=32 * rows * wide, transcendentals=0
        ),
        name="assemble",
    )


def matmul_sum(source, pieces):
    deep = pieces[0].shape[0]
    total = None
    for index, piece in enumerate(pieces):
        term = jnp.dot(
            source[:, index * deep : (index + 1) * deep],
            piece[...],
            preferred_element_type=jnp.float32,
        )
        total = term if total is None else total + term
    return total


def project(source, pieces, state=None, rows=256):
    tokens_here, depth = source.shape
    width = pieces[0].shape[1]
    count = len(pieces)

    def kernel(source_ref, *refs):
        total = matmul_sum(source_ref, refs[:count])
        if state is not None:
            slabs = [refs[count][j] for j in range(width // LANES)]
            total = jax.nn.gelu(total) * jnp.concatenate(slabs, axis=1)
        refs[-1][...] = total.astype(jnp.bfloat16)

    specs = [pl.BlockSpec((rows, depth), lambda i: (i, 0))]
    specs += [pl.BlockSpec(p.shape, lambda i: (0, 0)) for p in pieces]
    operands = [source, *pieces]
    if state is not None:
        specs.append(pl.BlockSpec((width // LANES, rows, LANES), lambda i: (0, i, 0)))
        operands.append(state)
    return pl.pallas_call(
        kernel,
        grid=(tokens_here // rows,),
        out_shape=jax.ShapeDtypeStruct((tokens_here, width), jnp.bfloat16),
        in_specs=specs,
        out_specs=pl.BlockSpec((rows, width), lambda i: (i, 0)),
        compiler_params=pltpu.CompilerParams(vmem_limit_bytes=GRANT),
        cost_estimate=pl.CostEstimate(
            flops=2 * tokens_here * depth * width,
            bytes_accessed=2 * (tokens_here * depth + depth * width),
            transcendentals=0,
        ),
        name="project_x" if state is None else "project_y",
    )(*operands)


SUBS = 8
LANES = 128


def advance(decay, drive, cosine, sine, real, imag):
    return (
        decay * (cosine * real - sine * imag) + drive,
        decay * (sine * real + cosine * imag),
    )


def expm1(value):
    near = 1.0 + value * (1.0 / 9.0)
    for k in range(8, 1, -1):
        near = 1.0 + (value * (1.0 / k)) * near
    return jnp.where(value > -0.5, value * near, jnp.exp(value) - 1.0)


def spread_lanes(table_ref, row):
    size = table_ref.shape[1]
    return [
        jnp.broadcast_to(table_ref[row : row + 1, j : j + LANES], (SUBS, LANES))
        for j in range(0, size, LANES)
    ]


def run_gates(place, x_proj, halo, table, decay_gate, input_gate, taps):
    tokens_here, width = x_proj.shape
    size = decay_gate.shape[1]
    heads = width // size
    length = tokens_here // 2
    part = length // SUBS

    def kernel(
        place_ref, x_ref, halo_ref, table_ref, decay_w, input_w,
        decay_ref, drive_ref, part_ref, total_ref, padded,
    ):
        edge = halo_ref.shape[1]
        padded[0:8, :] = halo_ref[0, edge - 8 : edge, :].astype(jnp.float32)
        padded[8 : 8 + length, :] = x_ref[...].astype(jnp.float32)
        convolved = table_ref[taps : taps + 1, :] + jnp.zeros((length, size), jnp.float32)
        for k in range(taps):
            convolved = convolved + table_ref[k : k + 1, :] * padded[8 - k : 8 - k + length, :]
        convolved = convolved.astype(jnp.bfloat16)
        rate = jax.nn.sigmoid(
            jnp.dot(convolved, decay_w[0], preferred_element_type=jnp.float32)
            + table_ref[taps + 1 : taps + 2, :]
        )
        opened = jax.nn.sigmoid(
            jnp.dot(convolved, input_w[0], preferred_element_type=jnp.float32)
            + table_ref[taps + 2 : taps + 3, :]
        )
        log_decay = rate * table_ref[taps + 3 : taps + 4, :]
        decay = jnp.exp(log_decay)
        drive = jnp.sqrt(-expm1(2.0 * log_decay)) * opened * convolved.astype(jnp.float32)
        for j in range(size // LANES):
            decay_ref[j] = decay[:, j * LANES : (j + 1) * LANES]
            drive_ref[j] = drive[:, j * LANES : (j + 1) * LANES]
        cosines = spread_lanes(table_ref, taps + 4)
        sines = spread_lanes(table_ref, taps + 5)

        def step(t, carry):
            after = []
            for j, (real, imag, product) in enumerate(carry):
                here = decay_ref[j, pl.ds(t, SUBS, stride=part), :]
                push = drive_ref[j, pl.ds(t, SUBS, stride=part), :]
                real, imag = advance(here, push, cosines[j], sines[j], real, imag)
                after.append((real, imag, product * here))
            return tuple(after)

        zeros = jnp.zeros((SUBS, LANES), jnp.float32)
        ends = lax.fori_loop(
            0, part, step, ((zeros, zeros, zeros + 1.0),) * (size // LANES), unroll=8
        )
        real, imag, product = (jnp.concatenate(rows, axis=1) for rows in zip(*ends))
        part_ref[0, 0:SUBS, :] = real
        part_ref[0, SUBS : 2 * SUBS, :] = imag
        part_ref[0, 2 * SUBS : 3 * SUBS, :] = product
        turn_cos, turn_sin = table_ref[taps + 6 : taps + 7, :], table_ref[taps + 7 : taps + 8, :]
        end_real, end_imag = real[0:1], imag[0:1]
        whole = product[0:1]
        for j in range(1, SUBS):
            here = product[j : j + 1]
            end_real, end_imag = (
                here * (turn_cos * end_real - turn_sin * end_imag) + real[j : j + 1],
                here * (turn_sin * end_real + turn_cos * end_imag) + imag[j : j + 1],
            )
            whole = whole * here
        total_ref[0, 0:1, :] = end_real
        total_ref[0, 1:2, :] = end_imag
        total_ref[0, 2:3, :] = whole
        total_ref[0, 3:8, :] = jnp.zeros((5, size), jnp.float32)

    depth = table.shape[0]
    lines = halo.shape[1]
    grid_spec = pltpu.PrefetchScalarGridSpec(
        num_scalar_prefetch=1,
        grid=(heads, 2),
        in_specs=[
            pl.BlockSpec((length, size), lambda h, r, p: (r, h)),
            pl.BlockSpec((1, lines, size), lambda h, r, p: (r, 0, h)),
            pl.BlockSpec((depth, size), lambda h, r, p: (0, p[4] * heads + h)),
            pl.BlockSpec((1, size, size), lambda h, r, p: (p[4] * heads + h, 0, 0)),
            pl.BlockSpec((1, size, size), lambda h, r, p: (p[4] * heads + h, 0, 0)),
        ],
        out_specs=[
            pl.BlockSpec((size // LANES, length, LANES), lambda h, r, p: (h, r, 0)),
            pl.BlockSpec((size // LANES, length, LANES), lambda h, r, p: (h, r, 0)),
            pl.BlockSpec((1, 3 * SUBS, size), lambda h, r, p: (r, 0, h)),
            pl.BlockSpec((1, 8, size), lambda h, r, p: (r, 0, h)),
        ],
        scratch_shapes=[pltpu.VMEM((length + 8, size), jnp.float32)],
    )
    return pl.pallas_call(
        kernel,
        grid_spec=grid_spec,
        out_shape=[
            jax.ShapeDtypeStruct((width // LANES, tokens_here, LANES), jnp.float32),
            jax.ShapeDtypeStruct((width // LANES, tokens_here, LANES), jnp.float32),
            jax.ShapeDtypeStruct((2, 3 * SUBS, width), jnp.float32),
            jax.ShapeDtypeStruct((2, 8, width), jnp.float32),
        ],
        compiler_params=pltpu.CompilerParams(vmem_limit_bytes=GRANT),
        cost_estimate=pl.CostEstimate(
            flops=4 * tokens_here * width * size,
            bytes_accessed=10 * tokens_here * width,
            transcendentals=8 * tokens_here * width,
        ),
        name="gates",
    )(place, x_proj, halo, table, decay_gate, input_gate)


def run_states(place, decay, drive, parts, totals, table, taps, size, outer, highs):
    tokens_here, width = decay.shape[1], decay.shape[0] * LANES
    heads = width // size
    length = tokens_here // 2
    part = length // SUBS

    def kernel(place_ref, decay_ref, drive_ref, part_ref, total_ref, table_ref, state_ref, starts):
        x, high = place_ref[3], place_ref[5]
        run = pl.program_id(1)
        mine = (x * 2 + run) * highs + high

        def row(k):
            return table_ref[taps + k : taps + k + 1, :]

        far_cos, far_sin = row(8), row(9)
        real = jnp.zeros((1, size), jnp.float32)
        imag = jnp.zeros((1, size), jnp.float32)
        for q in range(outer * 2 * highs):
            at_x, at_run, at_high = q // (2 * highs), q // highs % 2, q % highs
            slot = (x ^ at_x) * highs + (high ^ at_high)
            rows = total_ref[slot * 2 + at_run]
            here = rows[2:3]
            new_real = here * (far_cos * real - far_sin * imag) + rows[0:1]
            new_imag = here * (far_sin * real + far_cos * imag) + rows[1:2]
            before = q < mine
            real = jnp.where(before, new_real, real)
            imag = jnp.where(before, new_imag, imag)
        turn_cos, turn_sin = row(6), row(7)
        for j in range(SUBS):
            starts[j : j + 1, :] = real
            starts[SUBS + j : SUBS + j + 1, :] = imag
            here = part_ref[0, 2 * SUBS + j : 2 * SUBS + j + 1, :]
            real, imag = (
                here * (turn_cos * real - turn_sin * imag) + part_ref[0, j : j + 1, :],
                here * (turn_sin * real + turn_cos * imag)
                + part_ref[0, SUBS + j : SUBS + j + 1, :],
            )
        cosines = spread_lanes(table_ref, taps + 4)
        sines = spread_lanes(table_ref, taps + 5)

        def step(t, carry):
            after = []
            for j, (real, imag) in enumerate(carry):
                here = decay_ref[j, pl.ds(t, SUBS, stride=part), :]
                push = drive_ref[j, pl.ds(t, SUBS, stride=part), :]
                real, imag = advance(here, push, cosines[j], sines[j], real, imag)
                state_ref[j, pl.ds(t, SUBS, stride=part), :] = real
                after.append((real, imag))
            return tuple(after)

        begin = tuple(
            (starts[0:SUBS, j : j + LANES], starts[SUBS : 2 * SUBS, j : j + LANES])
            for j in range(0, size, LANES)
        )
        lax.fori_loop(0, part, step, begin, unroll=8)

    depth = table.shape[0]
    slots = totals.shape[0]
    grid_spec = pltpu.PrefetchScalarGridSpec(
        num_scalar_prefetch=1,
        grid=(heads, 2),
        in_specs=[
            pl.BlockSpec((size // LANES, length, LANES), lambda h, r, p: (h, r, 0)),
            pl.BlockSpec((size // LANES, length, LANES), lambda h, r, p: (h, r, 0)),
            pl.BlockSpec((1, 3 * SUBS, size), lambda h, r, p: (r, 0, h)),
            pl.BlockSpec((slots, 8, size), lambda h, r, p: (0, 0, h)),
            pl.BlockSpec((depth, size), lambda h, r, p: (0, p[4] * heads + h)),
        ],
        out_specs=pl.BlockSpec((size // LANES, length, LANES), lambda h, r, p: (h, r, 0)),
        scratch_shapes=[pltpu.VMEM((2 * SUBS, size), jnp.float32)],
    )
    return pl.pallas_call(
        kernel,
        grid_spec=grid_spec,
        out_shape=jax.ShapeDtypeStruct((width // LANES, tokens_here, LANES), jnp.float32),
        compiler_params=pltpu.CompilerParams(vmem_limit_bytes=GRANT),
        cost_estimate=pl.CostEstimate(
            flops=10 * tokens_here * width,
            bytes_accessed=12 * tokens_here * width,
            transcendentals=0,
        ),
        name="states",
    )(place, decay, drive, parts, totals, table)


def mix(place, gated, gated_other, pair):
    tokens_here, half = gated.shape
    width = pair[0].shape[1]

    def kernel(place_ref, own_ref, other_ref, first_ref, second_ref, leave_ref, stay_ref):
        c, turn = place_ref[0], place_ref[2]
        near = pl.multiple_of(c * half, half)
        far = pl.multiple_of((1 - c) * half, half)

        def product(weight_ref):
            return jnp.dot(
                own_ref[...], weight_ref[pl.ds(near, half), :], preferred_element_type=jnp.float32
            ) + jnp.dot(
                other_ref[...], weight_ref[pl.ds(far, half), :], preferred_element_type=jnp.float32
            )

        first = product(first_ref)
        second = product(second_ref)
        leave_ref[...] = jnp.where(turn == 0, second, first).astype(jnp.bfloat16)
        stay_ref[...] = jnp.where(turn == 0, first, second)

    rows = tokens_here // 4
    return pl.pallas_call(
        kernel,
        grid=(4,),
        out_shape=[
            jax.ShapeDtypeStruct((tokens_here, width), jnp.bfloat16),
            jax.ShapeDtypeStruct((tokens_here, width), jnp.float32),
        ],
        in_specs=[
            SMEM,
            pl.BlockSpec((rows, half), lambda i: (i, 0)),
            pl.BlockSpec((rows, half), lambda i: (i, 0)),
            pl.BlockSpec(pair[0].shape, lambda i: (0, 0)),
            pl.BlockSpec(pair[1].shape, lambda i: (0, 0)),
        ],
        out_specs=[
            pl.BlockSpec((rows, width), lambda i: (i, 0)),
            pl.BlockSpec((rows, width), lambda i: (i, 0)),
        ],
        compiler_params=pltpu.CompilerParams(vmem_limit_bytes=GRANT),
        cost_estimate=pl.CostEstimate(
            flops=8 * tokens_here * half * width,
            bytes_accessed=4 * tokens_here * half + 10 * tokens_here * width,
            transcendentals=0,
        ),
        name="mix",
    )(place, gated, gated_other, *pair)


def place_columns(place, own, other):
    rows, block = own[0].shape
    segs = len(own)

    def kernel(place_ref, *refs):
        c, z = place_ref[0], place_ref[1]
        whole = refs[-1]
        for b in range(segs):
            for d in range(2):
                at = pl.multiple_of(((c ^ d) * segs + (z ^ b)) * block, block)
                whole[:, pl.ds(at, block)] = refs[d * segs + b][...]

    return pl.pallas_call(
        kernel,
        out_shape=jax.ShapeDtypeStruct((rows, 2 * segs * block), own[0].dtype),
        in_specs=[SMEM] + [VMEM] * (2 * segs),
        out_specs=VMEM,
        name="place",
    )(place, *own, *other)


def folded(
    tokens,
    x_weight,
    y_weight,
    out_weight,
    conv_weight,
    conv_bias,
    decay_gate,
    decay_bias,
    input_gate,
    input_bias,
    log_rate,
    phase,
):
    grps, segs = lax.axis_size("grp"), lax.axis_size("seg")
    g, z, y = lax.axis_index("grp"), lax.axis_index("seg"), lax.axis_index("mp")
    outer, highs = grps // 2, segs // 2
    x, c = g // 2, g % 2
    high, low = z // 2, z % 2
    turn = x ^ y
    rows, wide = tokens.shape
    columns = x_weight.shape[1]
    width = columns // 4
    size = decay_gate.shape[1]
    taps = conv_weight.shape[0]
    length = 2 * rows
    place = jnp.stack([c, z, turn, x, low * 2 + c, high]).astype(jnp.int32)

    by_z = swap(tokens, "seg", 1)
    here = [tokens, swap(tokens, "mp", 1), by_z, swap(by_z, "mp", 1)]
    there = [swap(piece, "grp", 1) for piece in here]
    source = build_assemble(rows, wide, segs, tokens.dtype)(place, *here, *there)

    def cut(weight, at_low, at_c):
        return lax.dynamic_slice(
            weight, (0, at_low * (2 * width) + at_c * width), (weight.shape[0], width)
        )

    def columns_of(weight):
        leaving = jnp.concatenate([cut(weight, low, 1 - c), cut(weight, 1 - low, 1 - c)])
        arrived = swap(leaving, "grp", 1)
        deep = weight.shape[0]
        own = jnp.concatenate([cut(weight, low, c), arrived[:deep]])
        other = jnp.concatenate([cut(weight, 1 - low, c), arrived[deep:]])
        near, far = spread((own, other))
        return near + far

    half = 2 * width
    x_pieces = columns_of(x_weight)
    y_pieces = columns_of(y_weight)
    out_pieces = spread(
        (
            lax.dynamic_slice(out_weight, (low * half, 0), (half, out_weight.shape[1])),
            lax.dynamic_slice(out_weight, ((1 - low) * half, 0), (half, out_weight.shape[1])),
        ),
    )

    part = length // SUBS
    table = jnp.stack(
        [conv_weight[k] for k in range(taps)]
        + [
            conv_bias,
            decay_bias,
            input_bias,
            -8.0 * jax.nn.softplus(log_rate),
            jnp.cos(phase),
            jnp.sin(phase),
            jnp.cos(part * phase),
            jnp.sin(part * phase),
            jnp.cos(length * phase),
            jnp.sin(length * phase),
        ]
    )

    x_proj = project(source, x_pieces)

    lines = 16
    tails = jnp.stack([x_proj[length - lines : length], x_proj[2 * length - lines :]])
    cycle = [
        (zh * 2 + zl, (zh + 1) % highs * 2 + zl) for zh in range(highs) for zl in range(2)
    ]
    tail_z = lax.ppermute(tails, "seg", cycle)
    across = [
        (((ox * 2 + oc) * segs + (highs - 1) * 2 + zl), ((ox + 1) * 2 + oc) * segs + zl)
        for ox in range(outer - 1)
        for oc in range(2)
        for zl in range(2)
    ]
    tail_x = lax.ppermute(tails[1], ("grp", "seg"), across)
    first = high == 0
    halo = jnp.stack(
        [
            jnp.where(first, tail_x, tail_z[0]),
            jnp.where(first, tail_z[0], tail_z[1]),
        ]
    )

    decay, drive, parts, total = run_gates(
        place, x_proj, halo, table, decay_gate, input_gate, taps
    )
    totals = []
    for i in range(outer):
        for j in range(highs):
            if i == 0 and j == 0:
                totals.append(total)
                continue
            pairs = [
                (og * segs + oz, (og ^ (2 * i)) * segs + (oz ^ (2 * j)))
                for og in range(grps)
                for oz in range(segs)
            ]
            totals.append(lax.ppermute(total, ("grp", "seg"), pairs))
    state = run_states(
        place, decay, drive, parts, jnp.concatenate(totals), table, taps, size, outer, highs
    )

    gated = project(source, y_pieces, state)
    gated_other = swap(gated, "grp", 1)

    summed = []
    for b in range(segs):
        leave, stay = mix(place, gated, gated_other, (out_pieces[0][b], out_pieces[1][b]))
        summed.append(stay + swap(leave, "mp", 1).astype(jnp.float32))

    def rows_of(b, at_c, at_low):
        return lax.dynamic_slice(
            summed[b], (at_c * length + at_low * rows, 0), (rows, summed[b].shape[1])
        )

    own_blocks, other_blocks = [], []
    for b in range(segs):
        leaving = jnp.concatenate([rows_of(b ^ 1, 0, 1 - low), rows_of(b ^ 1, 1, 1 - low)])
        arrived = swap(leaving.astype(jnp.bfloat16), "seg", 1)

        def done(at_c):
            late = lax.dynamic_slice(arrived, (at_c * rows, 0), (rows, arrived.shape[1]))
            return (rows_of(b, at_c, low) + late.astype(jnp.float32)).astype(jnp.bfloat16)

        own_blocks.append(done(c))
        other_blocks.append(swap(done(1 - c), "grp", 1))
    return place_columns(place, own_blocks, other_blocks)


def solution(mesh):
    grps, segs, mps = mesh.shape["grp"], mesh.shape["seg"], mesh.shape["mp"]
    powers = segs >= 4 and segs & (segs - 1) == 0
    fits = grps == 2 * mps and mps == 2 and powers
    in_specs = (
        P(("grp", "seg"), "mp"),
        P(("grp", "seg"), "mp"),
        P(("grp", "seg"), "mp"),
        P("mp", ("grp", "seg")),
        P(None, "mp"),
        P("mp"),
        P("mp", None, None),
        P("mp"),
        P("mp", None, None),
        P("mp"),
        P("mp"),
        P("mp"),
    )
    out_specs = P(("grp", "seg"), "mp")
    local = folded if fits else general
    return jax.shard_map(local, mesh=mesh, in_specs=in_specs, out_specs=out_specs, check_vma=False)
```

```python
import jax
import jax.numpy as jnp
from jax import lax
from jax.experimental import pallas as pl
from jax.experimental.pallas import tpu as pltpu
from jax.sharding import PartitionSpec as P


VMEM = pl.BlockSpec(memory_space=pltpu.VMEM)
SMEM = pl.BlockSpec(memory_space=pltpu.SMEM)
GRANT = 56 * 1024 * 1024


def shifted(value, axis, by):
    peers = lax.axis_size(axis)
    pairs = [(i, i + by) for i in range(peers) if 0 <= i + by < peers]
    return lax.ppermute(value, axis, pairs)


def carried_in(value, axis, join, neutral):
    count, mine = (lax.axis_size(axis), lax.axis_index(axis))
    pieces = lax.all_gather(value, axis)
    total = jnp.full_like(value, 0) + jnp.asarray(neutral, value.dtype)

    def turn(position, total):
        longer = join(total, pieces[position])
        return jnp.where(position < mine, longer, total)

    return lax.fori_loop(0, count - 1, turn, total)


def combine(earlier, later):
    first_real = earlier[0] * later[0] - earlier[1] * later[1]
    first_imag = earlier[0] * later[1] + earlier[1] * later[0]
    state_real = later[0] * earlier[2] - later[1] * earlier[3] + later[2]
    state_imag = later[0] * earlier[3] + later[1] * earlier[2] + later[3]
    return jnp.stack([first_real, first_imag, state_real, state_imag])


def neutral(count):
    ones_row = jnp.ones((count,), jnp.float32)
    zeros_row = jnp.zeros((count,), jnp.float32)
    return jnp.stack([ones_row, zeros_row, zeros_row, zeros_row])


def general(
    tokens,
    x_weight,
    y_weight,
    out_weight,
    conv_weight,
    conv_bias,
    decay_gate,
    decay_bias,
    input_gate,
    input_bias,
    log_rate,
    phase,
):
    source = lax.all_gather(tokens, "mp", axis=1, tiled=True)
    tokens_here = source.shape[0]
    width = x_weight.shape[1]

    def add_rows(shard_piece):
        return jnp.dot(source, shard_piece, preferred_element_type=jnp.float32)

    x_sum = add_rows(lax.all_gather(x_weight, ("grp", "seg"), axis=0, tiled=True))
    y_sum = add_rows(lax.all_gather(y_weight, ("grp", "seg"), axis=0, tiled=True))
    x_proj = x_sum.astype(jnp.bfloat16)
    branch = jax.nn.gelu(y_sum)
    taps = conv_weight.shape[0]
    last_rows = x_proj[tokens_here - (taps - 1) :]
    before = shifted(last_rows, ("grp", "seg"), 1)
    padded = jnp.concatenate([before, x_proj], axis=0).astype(jnp.float32)
    convolved = conv_bias + jnp.zeros((tokens_here, width), jnp.float32)
    for offset in range(taps):
        convolved = (
            convolved
            + conv_weight[offset] * padded[taps - 1 - offset : taps - 1 - offset + tokens_here]
        )
    convolved = convolved.astype(jnp.bfloat16)
    heads_here = decay_gate.shape[0]
    block_size = decay_gate.shape[1]
    head_view = convolved.reshape(tokens_here, heads_here, block_size)
    rate_gate = jax.nn.sigmoid(
        jnp.einsum(
            "nhd,hde->nhe", head_view, decay_gate, preferred_element_type=jnp.float32
        ).reshape(tokens_here, width)
        + decay_bias
    )
    input_open = jax.nn.sigmoid(
        jnp.einsum(
            "nhd,hde->nhe", head_view, input_gate, preferred_element_type=jnp.float32
        ).reshape(tokens_here, width)
        + input_bias
    )
    log_decay = -8.0 * rate_gate * jax.nn.softplus(log_rate)
    decay = jnp.exp(log_decay)
    drive = jnp.sqrt(-jnp.expm1(2.0 * log_decay)) * input_open * convolved.astype(jnp.float32)
    elements = jnp.stack(
        [decay * jnp.cos(phase), decay * jnp.sin(phase), drive, jnp.zeros_like(drive)]
    )
    running = lax.associative_scan(combine, elements, axis=1)
    summary = running[:, tokens_here - 1]
    identity = neutral(width)
    carry_in = carried_in(summary, ("grp", "seg"), combine, identity)
    state_real = running[2] + running[0] * carry_in[2] - running[1] * carry_in[3]
    gated = (branch * state_real).astype(jnp.bfloat16)
    partial_value = jnp.dot(
        gated,
        lax.all_gather(out_weight, ("grp", "seg"), axis=1, tiled=True),
        preferred_element_type=jnp.float32,
    )
    reduced = lax.psum_scatter(
        partial_value.astype(jnp.bfloat16), "mp", scatter_dimension=1, tiled=True
    )
    return reduced


def swap(value, axis, bit):
    count = lax.axis_size(axis)
    return lax.ppermute(value, axis, [(i, i ^ bit) for i in range(count)])


def spread(own, other):
    near = [own]
    for b in range(1, lax.axis_size("seg")):
        near.append(swap(other if b % 2 else own, "seg", b))
    return near, [swap(piece, "grp", 2) for piece in near]


def assemble(place, pieces, segs):
    rows, wide = pieces[0].shape
    lows = len(pieces) // 4
    block = wide // 2 // segs

    def kernel(place_ref, *refs):
        c, z, turn, low = place_ref[0], place_ref[1], place_ref[2], place_ref[6]
        for b in range(segs):
            for d in range(2):
                source = pl.multiple_of(((c ^ d) * segs + (z ^ b)) * block, block)
                for index, piece in enumerate(refs[:-1]):
                    e, f, h = index // (2 * lows), index // 2 % lows, index % 2
                    at_low = low ^ f if lows == 2 else 0
                    row = pl.multiple_of(((c ^ e) * lows + at_low) * rows, rows)
                    column = pl.multiple_of((turn ^ h) * wide + (b * 2 + d) * block, block)
                    refs[-1][pl.ds(row, rows), pl.ds(column, block)] = piece[
                        :, pl.ds(source, block)
                    ]

    return pl.pallas_call(
        kernel,
        out_shape=jax.ShapeDtypeStruct((2 * lows * rows, 2 * wide), pieces[0].dtype),
        in_specs=[SMEM] + [VMEM] * len(pieces),
        out_specs=VMEM,
        compiler_params=pltpu.CompilerParams(vmem_limit_bytes=GRANT),
        cost_estimate=pl.CostEstimate(
            flops=0, bytes_accessed=4 * len(pieces) * rows * wide, transcendentals=0
        ),
        name="set_together",
    )(place, *pieces)


def matmul_sum(source, pieces):
    deep = pieces[0].shape[0]
    total = None
    for index, piece in enumerate(pieces):
        term = jnp.dot(
            source[:, index * deep : (index + 1) * deep],
            piece[...],
            preferred_element_type=jnp.float32,
        )
        total = term if total is None else total + term
    return total


def project(source, half, pieces, edge=None, before=None, state=None, last=True, rows=256):
    tokens_here = source.shape[0]
    depth = source.shape[1] // 2
    width = pieces[0].shape[1]
    count = len(pieces)
    kind = jnp.bfloat16 if last else jnp.float32

    def row_block(i):
        return (i, 0)

    def whole(i):
        return (0, 0)

    specs = [pl.BlockSpec((rows, depth), lambda i: (i, half))]
    specs += [pl.BlockSpec(p.shape, whole) for p in pieces]
    operands = [source, *pieces]
    out_specs = [pl.BlockSpec((rows, width), row_block)]
    out_shape = [jax.ShapeDtypeStruct((tokens_here, width), kind)]
    if before is not None:
        specs.append(pl.BlockSpec((rows, width), row_block))
        operands.append(before)
    if state is not None:
        specs.append(pl.BlockSpec((width // LANES, rows, LANES), lambda i: (0, i, 0)))
        operands.append(state)
    if edge is not None:
        short, others = edge
        specs += [pl.BlockSpec(a.shape, whole) for a in (short, *others)]
        operands += [short, *others]
        out_specs.append(pl.BlockSpec((short.shape[0], width), whole))
        out_shape.append(jax.ShapeDtypeStruct((short.shape[0], width), kind))
    outs = len(out_shape)

    def kernel(source_ref, *refs):
        weights, extra, out = refs[:count], list(refs[count:-outs]), refs[-outs:]
        total = matmul_sum(source_ref, weights)
        if before is not None:
            total = total + extra.pop(0)[...]
        if state is not None:
            state_ref = extra.pop(0)
            slabs = [state_ref[j] for j in range(width // LANES)]
            total = jax.nn.gelu(total) * jnp.concatenate(slabs, axis=1)
        out[0][...] = total.astype(kind)
        if edge is not None:

            @pl.when(pl.program_id(0) == 0)
            def edge_rows():
                short_ref = extra[0]
                halves = [short_ref.at[:, k * depth : (k + 1) * depth] for k in range(2)]
                ends = matmul_sum(halves[half], weights) + matmul_sum(halves[1 - half], extra[1:])
                out[1][...] = ends.astype(kind)

    return pl.pallas_call(
        kernel,
        grid=(tokens_here // rows,),
        out_shape=out_shape,
        in_specs=specs,
        out_specs=out_specs,
        compiler_params=pltpu.CompilerParams(vmem_limit_bytes=GRANT),
        cost_estimate=pl.CostEstimate(
            flops=2 * tokens_here * depth * width,
            bytes_accessed=2 * (tokens_here * depth + depth * width),
            transcendentals=0,
        ),
        name="project",
    )(*operands)


SUBS = 8
LANES = 128


def advance(decay, drive, cosine, sine, real, imag):
    return (
        decay * (cosine * real - sine * imag) + drive,
        decay * (sine * real + cosine * imag),
    )


def expm1(value):
    near = 1.0 + value * (1.0 / 9.0)
    for k in range(8, 1, -1):
        near = 1.0 + (value * (1.0 / k)) * near
    return jnp.where(value > -0.5, value * near, jnp.exp(value) - 1.0)


def spread_lanes(table_ref, row):
    size = table_ref.shape[1]
    return [
        jnp.broadcast_to(table_ref[row : row + 1, j : j + LANES], (SUBS, LANES))
        for j in range(0, size, LANES)
    ]


def decay_and_drive(convolved, decay_w, input_w, table_ref, taps):
    convolved = convolved.astype(jnp.bfloat16)
    rate = jax.nn.sigmoid(
        jnp.dot(convolved, decay_w[0], preferred_element_type=jnp.float32)
        + table_ref[taps + 1 : taps + 2, :]
    )
    opened = jax.nn.sigmoid(
        jnp.dot(convolved, input_w[0], preferred_element_type=jnp.float32)
        + table_ref[taps + 2 : taps + 3, :]
    )
    log_decay = rate * table_ref[taps + 3 : taps + 4, :]
    drive = jnp.sqrt(-expm1(2.0 * log_decay)) * opened * convolved.astype(jnp.float32)
    return jnp.exp(log_decay), drive


def run_gates(place, x_proj, table, decay_gate, input_gate, taps):
    tokens_here, width = x_proj.shape
    size = decay_gate.shape[1]
    heads = width // size
    length = tokens_here // 2
    part = length // SUBS

    def kernel(
        place_ref, x_ref, table_ref, decay_w, input_w,
        decay_ref, drive_ref, part_ref, total_ref, padded,
    ):
        padded[0:8, :] = jnp.zeros((8, size), jnp.float32)
        padded[8 : 8 + length, :] = x_ref[...].astype(jnp.float32)
        convolved = table_ref[taps : taps + 1, :] + jnp.zeros((length, size), jnp.float32)
        for k in range(taps):
            convolved = convolved + table_ref[k : k + 1, :] * padded[8 - k : 8 - k + length, :]
        decay, drive = decay_and_drive(convolved, decay_w, input_w, table_ref, taps)
        for j in range(size // LANES):
            decay_ref[j] = decay[:, j * LANES : (j + 1) * LANES]
            drive_ref[j] = drive[:, j * LANES : (j + 1) * LANES]
            decay_ref[j, 0 : taps - 1, :] = jnp.ones((taps - 1, LANES), jnp.float32)
            drive_ref[j, 0 : taps - 1, :] = jnp.zeros((taps - 1, LANES), jnp.float32)
        cosines = spread_lanes(table_ref, taps + 4)
        sines = spread_lanes(table_ref, taps + 5)

        def step(t, carry):
            after = []
            for j, (real, imag, product) in enumerate(carry):
                here = decay_ref[j, pl.ds(t, SUBS, stride=part), :]
                push = drive_ref[j, pl.ds(t, SUBS, stride=part), :]
                real, imag = advance(here, push, cosines[j], sines[j], real, imag)
                after.append((real, imag, product * here))
            return tuple(after)

        zeros = jnp.zeros((SUBS, LANES), jnp.float32)
        ends = lax.fori_loop(
            0, part, step, ((zeros, zeros, zeros + 1.0),) * (size // LANES), unroll=8
        )
        real, imag, product = (jnp.concatenate(rows, axis=1) for rows in zip(*ends))
        part_ref[0, 0:SUBS, :] = real
        part_ref[0, SUBS : 2 * SUBS, :] = imag
        part_ref[0, 2 * SUBS : 3 * SUBS, :] = product
        turn_cos, turn_sin = table_ref[taps + 6 : taps + 7, :], table_ref[taps + 7 : taps + 8, :]
        end_real, end_imag = real[0:1], imag[0:1]
        whole = product[0:1]
        for j in range(1, SUBS):
            here = product[j : j + 1]
            end_real, end_imag = (
                here * (turn_cos * end_real - turn_sin * end_imag) + real[j : j + 1],
                here * (turn_sin * end_real + turn_cos * end_imag) + imag[j : j + 1],
            )
            whole = whole * here
        total_ref[0, 0:1, :] = end_real
        total_ref[0, 1:2, :] = end_imag
        total_ref[0, 2:3, :] = whole
        total_ref[0, 3:8, :] = padded[8:13, :]
        total_ref[0, 8:16, :] = padded[length : length + 8, :]

    depth = table.shape[0]
    grid_spec = pltpu.PrefetchScalarGridSpec(
        num_scalar_prefetch=1,
        grid=(heads, 2),
        in_specs=[
            pl.BlockSpec((length, size), lambda h, r, p: (r, h)),
            pl.BlockSpec((depth, size), lambda h, r, p: (0, p[4] * heads + h)),
            pl.BlockSpec((1, size, size), lambda h, r, p: (p[4] * heads + h, 0, 0)),
            pl.BlockSpec((1, size, size), lambda h, r, p: (p[4] * heads + h, 0, 0)),
        ],
        out_specs=[
            pl.BlockSpec((size // LANES, length, LANES), lambda h, r, p: (h, r, 0)),
            pl.BlockSpec((size // LANES, length, LANES), lambda h, r, p: (h, r, 0)),
            pl.BlockSpec((1, 3 * SUBS, size), lambda h, r, p: (r, 0, h)),
            pl.BlockSpec((1, 16, size), lambda h, r, p: (r, 0, h)),
        ],
        scratch_shapes=[pltpu.VMEM((length + 8, size), jnp.float32)],
    )
    return pl.pallas_call(
        kernel,
        grid_spec=grid_spec,
        out_shape=[
            jax.ShapeDtypeStruct((width // LANES, tokens_here, LANES), jnp.float32),
            jax.ShapeDtypeStruct((width // LANES, tokens_here, LANES), jnp.float32),
            jax.ShapeDtypeStruct((2, 3 * SUBS, width), jnp.float32),
            jax.ShapeDtypeStruct((2, 16, width), jnp.float32),
        ],
        compiler_params=pltpu.CompilerParams(vmem_limit_bytes=GRANT),
        cost_estimate=pl.CostEstimate(
            flops=4 * tokens_here * width * size,
            bytes_accessed=10 * tokens_here * width,
            transcendentals=8 * tokens_here * width,
        ),
        name="gates",
    )(place, x_proj, table, decay_gate, input_gate)


def run_states(
    place, decay, drive, parts, totals, table, decay_gate, input_gate, taps, outer, highs
):
    tokens_here, width = decay.shape[1], decay.shape[0] * LANES
    size = decay_gate.shape[1]
    heads = width // size
    length = tokens_here // 2
    part = length // SUBS
    first = taps - 1
    runs = outer * 2 * highs

    def kernel(
        place_ref, decay_ref, drive_ref, part_ref, total_ref, table_ref, decay_w, input_w,
        state_ref, starts, begin, rows_ref, early_decay, early_drive,
    ):
        x, high = place_ref[3], place_ref[5]
        run = pl.program_id(1)

        def row(k):
            return table_ref[taps + k : taps + k + 1, :]

        def turned(here, cosine, sine, real, imag, add_real, add_imag):
            return (
                here * (cosine * real - sine * imag) + add_real,
                here * (sine * real + cosine * imag) + add_imag,
            )

        def begun(base, real, imag):
            here, push = early_decay[pl.ds(base, 8), :], early_drive[pl.ds(base, 8), :]
            for t in range(first):
                real, imag = turned(
                    here[t : t + 1], row(4), row(5), real, imag, push[t : t + 1], 0.0
                )
            return real, imag

        def slot(q):
            at_x, at_run, at_high = q // (2 * highs), q // highs % 2, q % highs
            return ((x ^ at_x) * highs + (high ^ at_high)) * 2 + at_run

        @pl.when(run == 0)
        def every_run():
            zeros = jnp.zeros((8, size), jnp.float32)
            for q in range(runs):
                mine = total_ref[slot(q)]
                if q == 0:
                    rows_ref[0:8, :] = zeros
                else:
                    rows_ref[0:8, :] = total_ref[slot(q - 1)][8:16]
                rows_ref[8:16, :] = zeros
                rows_ref[8 : 8 + first, :] = mine[3 : 3 + first]
                convolved = row(0) + zeros
                for k in range(taps):
                    convolved = convolved + table_ref[k : k + 1, :] * rows_ref[8 - k : 16 - k, :]
                early_drive[q * 8 : q * 8 + 8, :] = convolved
            here, push = decay_and_drive(early_drive[...], decay_w, input_w, table_ref, taps)
            early_decay[...] = here
            early_drive[...] = push
            real = jnp.zeros((1, size), jnp.float32)
            imag = jnp.zeros((1, size), jnp.float32)
            for q in range(runs):
                at_run = q // highs % 2
                ours = (x == q // (2 * highs)) & (high == q % highs)

                @pl.when(ours)
                def keep():
                    begin[8 * at_run : 8 * at_run + 1, :] = real
                    begin[8 * at_run + 1 : 8 * at_run + 2, :] = imag

                if q < runs - 1:
                    mine = total_ref[slot(q)]
                    real, imag = begun(q * 8, real, imag)
                    real, imag = turned(
                        mine[2:3], row(8), row(9), real, imag, mine[0:1], mine[1:2]
                    )

        base = pl.multiple_of(((x * 2 + run) * highs + high) * 8, 8)
        kept = begin[pl.ds(pl.multiple_of(run * 8, 8), 8), :]
        real, imag = kept[0:1], kept[1:2]
        early_here, early_push = early_decay[pl.ds(base, 8), :], early_drive[pl.ds(base, 8), :]
        for j in range(SUBS):
            starts[j : j + 1, :] = real
            starts[SUBS + j : SUBS + j + 1, :] = imag
            if j == 0:
                real, imag = begun(base, real, imag)
            spin = row(10), row(11)
            if j > 0:
                spin = row(6), row(7)
            real, imag = turned(
                part_ref[0, 2 * SUBS + j : 2 * SUBS + j + 1, :], *spin, real, imag,
                part_ref[0, j : j + 1, :], part_ref[0, SUBS + j : SUBS + j + 1, :],
            )
        cosines = spread_lanes(table_ref, taps + 4)
        sines = spread_lanes(table_ref, taps + 5)
        top = lax.broadcasted_iota(jnp.int32, (SUBS, LANES), 0) == 0

        def step(t, carry, early=False):
            after = []
            for j, (real, imag) in enumerate(carry):
                here = decay_ref[j, pl.ds(t, SUBS, stride=part), :]
                push = drive_ref[j, pl.ds(t, SUBS, stride=part), :]
                if early:
                    lanes = slice(j * LANES, (j + 1) * LANES)
                    here = jnp.where(top, early_here[t : t + 1, lanes], here)
                    push = jnp.where(top, early_push[t : t + 1, lanes], push)
                real, imag = advance(here, push, cosines[j], sines[j], real, imag)
                state_ref[j, pl.ds(t, SUBS, stride=part), :] = real
                after.append((real, imag))
            return tuple(after)

        carry = tuple(
            (starts[0:SUBS, j : j + LANES], starts[SUBS : 2 * SUBS, j : j + LANES])
            for j in range(0, size, LANES)
        )
        for t in range(8):
            carry = step(t, carry, t < first)
        lax.fori_loop(8, part, step, carry, unroll=8)

    depth = table.shape[0]
    slots = totals.shape[0]
    grid_spec = pltpu.PrefetchScalarGridSpec(
        num_scalar_prefetch=1,
        grid=(heads, 2),
        in_specs=[
            pl.BlockSpec((size // LANES, length, LANES), lambda h, r, p: (h, r, 0)),
            pl.BlockSpec((size // LANES, length, LANES), lambda h, r, p: (h, r, 0)),
            pl.BlockSpec((1, 3 * SUBS, size), lambda h, r, p: (r, 0, h)),
            pl.BlockSpec((slots, 16, size), lambda h, r, p: (0, 0, h)),
            pl.BlockSpec((depth, size), lambda h, r, p: (0, p[4] * heads + h)),
            pl.BlockSpec((1, size, size), lambda h, r, p: (p[4] * heads + h, 0, 0)),
            pl.BlockSpec((1, size, size), lambda h, r, p: (p[4] * heads + h, 0, 0)),
        ],
        out_specs=pl.BlockSpec((size // LANES, length, LANES), lambda h, r, p: (h, r, 0)),
        scratch_shapes=[
            pltpu.VMEM((2 * SUBS, size), jnp.float32),
            pltpu.VMEM((16, size), jnp.float32),
            pltpu.VMEM((16, size), jnp.float32),
            pltpu.VMEM((runs * 8, size), jnp.float32),
            pltpu.VMEM((runs * 8, size), jnp.float32),
        ],
    )
    return pl.pallas_call(
        kernel,
        grid_spec=grid_spec,
        out_shape=jax.ShapeDtypeStruct((width // LANES, tokens_here, LANES), jnp.float32),
        compiler_params=pltpu.CompilerParams(vmem_limit_bytes=GRANT),
        cost_estimate=pl.CostEstimate(
            flops=10 * tokens_here * width,
            bytes_accessed=12 * tokens_here * width,
            transcendentals=0,
        ),
        name="states",
    )(place, decay, drive, parts, totals, table, decay_gate, input_gate)


def products(c, gated, weights):
    deep = gated[0].shape[1]
    spots = [pl.multiple_of((c ^ e) * deep, deep) for e in range(2)]
    blocks = []
    for weight in weights:
        terms = [
            jnp.dot(
                gated[e][...], weight[pl.ds(spots[e], deep), :], preferred_element_type=jnp.float32
            )
            for e in range(2)
        ]
        blocks.append(terms[0] + terms[1])
    return blocks


def mix_near(place, parts, pieces):
    tokens_here, deep = parts[0].shape
    width = pieces[0].shape[1]
    rows = tokens_here // 4
    count = len(pieces)

    def kernel(place_ref, *refs):
        blocks = products(place_ref[0], refs[:2], refs[2:-1])
        for b in range(count):
            refs[-1][:, b * width : (b + 1) * width] = blocks[b]

    return pl.pallas_call(
        kernel,
        grid=(4,),
        out_shape=jax.ShapeDtypeStruct((tokens_here, count * width), jnp.float32),
        in_specs=[SMEM]
        + [pl.BlockSpec((rows, deep), lambda i: (i, 0))] * 2
        + [pl.BlockSpec(piece.shape, lambda i: (0, 0)) for piece in pieces],
        out_specs=pl.BlockSpec((rows, count * width), lambda i: (i, 0)),
        compiler_params=pltpu.CompilerParams(vmem_limit_bytes=GRANT),
        cost_estimate=pl.CostEstimate(
            flops=4 * count * tokens_here * deep * width,
            bytes_accessed=4 * tokens_here * deep + 16 * count * rows * width,
            transcendentals=0,
        ),
        name="mix_near",
    )(place, *parts, *pieces)


def mix_far(place, parts, pieces, near, column):
    tokens_here, deep = parts[0].shape
    width = pieces[0].shape[1]
    rows = tokens_here // 4
    count = len(pieces)

    def kernel(place_ref, *refs):
        near_ref, leave_ref, stay_ref = refs[-3:]
        blocks = products(place_ref[0], refs[:2], refs[2:-3])
        blocks = [
            block + near_ref[:, b * width : (b + 1) * width] for b, block in enumerate(blocks)
        ]

        @pl.when(pl.program_id(1) == 0)
        def leave():
            for b in range(count):
                at = (count - 1 - b) * width
                leave_ref[:, at : at + width] = blocks[b].astype(jnp.bfloat16)

        @pl.when(pl.program_id(1) == 1)
        def stay():
            for b in range(count):
                stay_ref[:, b * width : (b + 1) * width] = blocks[b]

    def row(r, f, p):
        return r * 2 + (1 - f ^ p[6])

    grid_spec = pltpu.PrefetchScalarGridSpec(
        num_scalar_prefetch=1,
        grid=(2, 2),
        in_specs=[pl.BlockSpec((rows, deep), lambda r, f, p: (row(r, f, p), 0)) for _ in parts]
        + [pl.BlockSpec(piece.shape, lambda r, f, p: (0, 0)) for piece in pieces]
        + [pl.BlockSpec((rows, count * width), lambda r, f, p: (row(r, f, p), column))],
        out_specs=[pl.BlockSpec((rows, count * width), lambda r, f, p: (r, 0))] * 2,
    )
    return pl.pallas_call(
        kernel,
        grid_spec=grid_spec,
        out_shape=[
            jax.ShapeDtypeStruct((2 * rows, count * width), jnp.bfloat16),
            jax.ShapeDtypeStruct((2 * rows, count * width), jnp.float32),
        ],
        compiler_params=pltpu.CompilerParams(vmem_limit_bytes=GRANT),
        cost_estimate=pl.CostEstimate(
            flops=4 * count * tokens_here * deep * width,
            bytes_accessed=4 * tokens_here * deep + 28 * count * rows * width,
            transcendentals=0,
        ),
        name="mix_far",
    )(place, *parts, *pieces, near)


def place_columns(place, groups, own, other, block):
    rows = own[0].shape[0]
    segs = sum(len(group) for group in groups)

    def kernel(place_ref, *refs):
        c, z = place_ref[0], place_ref[1]
        whole = refs[-1]
        for i, group in enumerate(groups):
            for j, b in enumerate(group):
                for d in range(2):
                    at = pl.multiple_of(((c ^ d) * segs + (z ^ b)) * block, block)
                    from_ref = refs[d * len(groups) + i]
                    whole[:, pl.ds(at, block)] = from_ref[:, j * block : (j + 1) * block]

    return pl.pallas_call(
        kernel,
        out_shape=jax.ShapeDtypeStruct((rows, 2 * segs * block), own[0].dtype),
        in_specs=[SMEM] + [VMEM] * (2 * len(own)),
        out_specs=VMEM,
        name="place",
    )(place, *own, *other)


def folded(
    tokens,
    x_weight,
    y_weight,
    out_weight,
    conv_weight,
    conv_bias,
    decay_gate,
    decay_bias,
    input_gate,
    input_bias,
    log_rate,
    phase,
):
    grps, segs = lax.axis_size("grp"), lax.axis_size("seg")
    g, z, y = lax.axis_index("grp"), lax.axis_index("seg"), lax.axis_index("mp")
    outer, highs = grps // 2, segs // 2
    x, c = g // 2, g % 2
    high, low = z // 2, z % 2
    turn = x ^ y
    rows, _ = tokens.shape
    columns = x_weight.shape[1]
    width = columns // 4
    taps = conv_weight.shape[0]
    length = 2 * rows
    place = jnp.stack([c, z, turn, x, low * 2 + c, high, low]).astype(jnp.int32)

    part = length // SUBS

    def less(count):
        c_all, s_all = jnp.cos(count * phase), jnp.sin(count * phase)
        c_few, s_few = jnp.cos((taps - 1) * phase), jnp.sin((taps - 1) * phase)
        return c_all * c_few + s_all * s_few, s_all * c_few - c_all * s_few

    table = jnp.stack(
        [conv_weight[k] for k in range(taps)]
        + [
            conv_bias,
            decay_bias,
            input_bias,
            -8.0 * jax.nn.softplus(log_rate),
            jnp.cos(phase),
            jnp.sin(phase),
            jnp.cos(part * phase),
            jnp.sin(part * phase),
            *less(length),
            *less(part),
        ]
    )

    by_z = swap(tokens, "seg", 1)
    here = [tokens, swap(tokens, "mp", 1), by_z, swap(by_z, "mp", 1)]
    tied, table = lax.optimization_barrier((tokens, table))
    there = [swap(piece, "grp", 1) for piece in [tied] + here[1:]]

    source = assemble(place, here + there, segs)

    def cut(weight, at_low, at_c):
        return lax.dynamic_slice(
            weight, (0, at_low * (2 * width) + at_c * width), (weight.shape[0], width)
        )

    def columns_of(weight):
        leaving = jnp.concatenate([cut(weight, low, 1 - c), cut(weight, 1 - low, 1 - c)])
        arrived = swap(leaving, "grp", 1)
        deep = weight.shape[0]
        own = jnp.concatenate([cut(weight, low, c), arrived[:deep]])
        other = jnp.concatenate([cut(weight, 1 - low, c), arrived[deep:]])
        return spread(own, other)

    x_near, x_far = columns_of(x_weight)
    y_near, y_far = columns_of(y_weight)

    half = 2 * width
    out_columns = out_weight.shape[1]
    out_near, out_far = spread(
        lax.dynamic_slice(out_weight, (low * half, 0), (half, out_columns)),
        lax.dynamic_slice(out_weight, ((1 - low) * half, 0), (half, out_columns)),
    )
    diagonal = turn == 0
    out_pieces = []
    for mine, theirs in zip(out_near, out_far):
        kept = jnp.where(diagonal, mine, theirs)
        passed = jnp.where(diagonal, theirs, mine)
        out_pieces.append((kept, swap(passed, "mp", 1)))

    (x_part,) = project(source, 0, x_near, last=False)
    (x_proj,) = project(source, 1, x_far, before=x_part)
    (y_part,) = project(source, 0, y_near, last=False)

    decay, drive, parts, total = run_gates(
        place, x_proj, table, decay_gate, input_gate, taps
    )
    totals = [total] + [swap(total, "seg", 2 * j) for j in range(1, highs)]
    totals = jnp.stack(totals)
    totals = [totals] + [swap(totals, "grp", 2 * i) for i in range(1, outer)]
    totals = jnp.stack(totals).reshape(outer * highs * 2, *total.shape[1:])
    state = run_states(
        place, decay, drive, parts, totals, table, decay_gate, input_gate, taps, outer, highs
    )

    (gated,) = project(source, 1, y_far, before=y_part, state=state)
    gated_y = swap(gated, "mp", 1)
    gated_near = [gated, swap(gated, "grp", 1)]
    gated_far = [gated_y, swap(gated_y, "grp", 1)]
    nears = []
    for b in range(0, segs, 2):
        nears.append(mix_near(place, gated_near, [out_pieces[b][0], out_pieces[b + 1][0]]))

    groups = [(b, b + 1) for b in range(0, segs - 2, 2)] + [(segs - 2,), (segs - 1,)]
    stays, arrivals = [], {}
    for group in groups:
        name = group[0]
        pieces = [out_pieces[b][1] for b in group]
        leave, stay = mix_far(place, gated_far, pieces, nears[name // 2], name % 2)
        stays.append(stay)
        partner = name if len(group) == 2 else name ^ 1
        arrivals[partner] = swap(leave, "seg", 1)

    own_blocks, other_blocks = [], []
    for group, stay in zip(groups, stays):
        arrived = arrivals[group[0]]

        def done(at_c):
            shape = (rows, stay.shape[1])
            kept = lax.dynamic_slice(stay, (at_c * rows, 0), shape)
            late = lax.dynamic_slice(arrived, (at_c * rows, 0), shape)
            return (kept + late.astype(jnp.float32)).astype(jnp.bfloat16)

        own_blocks.append(done(c))
        other_blocks.append(swap(done(1 - c), "grp", 1))
    return place_columns(place, groups, own_blocks, other_blocks, out_columns)


def solution(mesh):
    grps, segs, mps = mesh.shape["grp"], mesh.shape["seg"], mesh.shape["mp"]
    powers = segs >= 4 and segs & (segs - 1) == 0
    fits = grps == 2 * mps and mps == 2 and powers
    in_specs = (
        P(("grp", "seg"), "mp"),
        P(("grp", "seg"), "mp"),
        P(("grp", "seg"), "mp"),
        P("mp", ("grp", "seg")),
        P(None, "mp"),
        P("mp"),
        P("mp", None, None),
        P("mp"),
        P("mp", None, None),
        P("mp"),
        P("mp"),
        P("mp"),
    )
    out_specs = P(("grp", "seg"), "mp")

    def local(*arrays):
        return (folded if fits else general)(*arrays)

    return jax.shard_map(local, mesh=mesh, in_specs=in_specs, out_specs=out_specs, check_vma=False)
```

```python
import jax
import jax.numpy as jnp
from jax import lax
from jax.experimental import pallas as pl
from jax.experimental.pallas import tpu as pltpu
from jax.sharding import PartitionSpec as P


VMEM = pl.BlockSpec(memory_space=pltpu.VMEM)
SMEM = pl.BlockSpec(memory_space=pltpu.SMEM)
GRANT = 56 * 1024 * 1024


def shifted(value, axis, by):
    peers = lax.axis_size(axis)
    pairs = [(i, i + by) for i in range(peers) if 0 <= i + by < peers]
    return lax.ppermute(value, axis, pairs)


def carried_in(value, axis, join, neutral):
    count, mine = (lax.axis_size(axis), lax.axis_index(axis))
    pieces = lax.all_gather(value, axis)
    total = jnp.full_like(value, 0) + jnp.asarray(neutral, value.dtype)

    def turn(position, total):
        longer = join(total, pieces[position])
        return jnp.where(position < mine, longer, total)

    return lax.fori_loop(0, count - 1, turn, total)


def combine(earlier, later):
    first_real = earlier[0] * later[0] - earlier[1] * later[1]
    first_imag = earlier[0] * later[1] + earlier[1] * later[0]
    state_real = later[0] * earlier[2] - later[1] * earlier[3] + later[2]
    state_imag = later[0] * earlier[3] + later[1] * earlier[2] + later[3]
    return jnp.stack([first_real, first_imag, state_real, state_imag])


def neutral(count):
    ones_row = jnp.ones((count,), jnp.float32)
    zeros_row = jnp.zeros((count,), jnp.float32)
    return jnp.stack([ones_row, zeros_row, zeros_row, zeros_row])


def general(
    tokens,
    x_weight,
    y_weight,
    out_weight,
    conv_weight,
    conv_bias,
    decay_gate,
    decay_bias,
    input_gate,
    input_bias,
    log_rate,
    phase,
):
    source = lax.all_gather(tokens, "mp", axis=1, tiled=True)
    tokens_here = source.shape[0]
    width = x_weight.shape[1]

    def add_rows(shard_piece):
        return jnp.dot(source, shard_piece, preferred_element_type=jnp.float32)

    x_sum = add_rows(lax.all_gather(x_weight, ("grp", "seg"), axis=0, tiled=True))
    y_sum = add_rows(lax.all_gather(y_weight, ("grp", "seg"), axis=0, tiled=True))
    x_proj = x_sum.astype(jnp.bfloat16)
    branch = jax.nn.gelu(y_sum)
    taps = conv_weight.shape[0]
    last_rows = x_proj[tokens_here - (taps - 1) :]
    before = shifted(last_rows, ("grp", "seg"), 1)
    padded = jnp.concatenate([before, x_proj], axis=0).astype(jnp.float32)
    convolved = conv_bias + jnp.zeros((tokens_here, width), jnp.float32)
    for offset in range(taps):
        convolved = (
            convolved
            + conv_weight[offset] * padded[taps - 1 - offset : taps - 1 - offset + tokens_here]
        )
    convolved = convolved.astype(jnp.bfloat16)
    heads_here = decay_gate.shape[0]
    block_size = decay_gate.shape[1]
    head_view = convolved.reshape(tokens_here, heads_here, block_size)
    rate_gate = jax.nn.sigmoid(
        jnp.einsum(
            "nhd,hde->nhe", head_view, decay_gate, preferred_element_type=jnp.float32
        ).reshape(tokens_here, width)
        + decay_bias
    )
    input_open = jax.nn.sigmoid(
        jnp.einsum(
            "nhd,hde->nhe", head_view, input_gate, preferred_element_type=jnp.float32
        ).reshape(tokens_here, width)
        + input_bias
    )
    log_decay = -8.0 * rate_gate * jax.nn.softplus(log_rate)
    decay = jnp.exp(log_decay)
    drive = jnp.sqrt(-jnp.expm1(2.0 * log_decay)) * input_open * convolved.astype(jnp.float32)
    elements = jnp.stack(
        [decay * jnp.cos(phase), decay * jnp.sin(phase), drive, jnp.zeros_like(drive)]
    )
    running = lax.associative_scan(combine, elements, axis=1)
    summary = running[:, tokens_here - 1]
    identity = neutral(width)
    carry_in = carried_in(summary, ("grp", "seg"), combine, identity)
    state_real = running[2] + running[0] * carry_in[2] - running[1] * carry_in[3]
    gated = (branch * state_real).astype(jnp.bfloat16)
    partial_value = jnp.dot(
        gated,
        lax.all_gather(out_weight, ("grp", "seg"), axis=1, tiled=True),
        preferred_element_type=jnp.float32,
    )
    reduced = lax.psum_scatter(
        partial_value.astype(jnp.bfloat16), "mp", scatter_dimension=1, tiled=True
    )
    return reduced


def swap(value, axis, bit):
    count = lax.axis_size(axis)
    return lax.ppermute(value, axis, [(i, i ^ bit) for i in range(count)])


def spread(own, other):
    near = [own]
    for b in range(1, lax.axis_size("seg")):
        near.append(swap(other if b % 2 else own, "seg", b))
    return near, [swap(piece, "grp", 2) for piece in near]


def assemble(place, pieces, segs):
    rows, wide = pieces[0].shape
    lows = len(pieces) // 4
    block = wide // 2 // segs

    def kernel(place_ref, *refs):
        c, z, turn, low = place_ref[0], place_ref[1], place_ref[2], place_ref[6]
        for b in range(segs):
            for d in range(2):
                source = pl.multiple_of(((c ^ d) * segs + (z ^ b)) * block, block)
                for index, piece in enumerate(refs[:-1]):
                    e, f, h = index // (2 * lows), index // 2 % lows, index % 2
                    at_low = low ^ f if lows == 2 else 0
                    row = pl.multiple_of(((c ^ e) * lows + at_low) * rows, rows)
                    column = pl.multiple_of((turn ^ h) * wide + (b * 2 + d) * block, block)
                    refs[-1][pl.ds(row, rows), pl.ds(column, block)] = piece[
                        :, pl.ds(source, block)
                    ]

    return pl.pallas_call(
        kernel,
        out_shape=jax.ShapeDtypeStruct((2 * lows * rows, 2 * wide), pieces[0].dtype),
        in_specs=[SMEM] + [VMEM] * len(pieces),
        out_specs=VMEM,
        compiler_params=pltpu.CompilerParams(vmem_limit_bytes=GRANT),
        cost_estimate=pl.CostEstimate(
            flops=0, bytes_accessed=4 * len(pieces) * rows * wide, transcendentals=0
        ),
        name="set_together",
    )(place, *pieces)


def matmul_sum(source, pieces):
    deep = pieces[0].shape[0]
    total = None
    for index, piece in enumerate(pieces):
        term = jnp.dot(
            source[:, index * deep : (index + 1) * deep],
            piece[...],
            preferred_element_type=jnp.float32,
        )
        total = term if total is None else total + term
    return total


def project(source, half, pieces, edge=None, before=None, state=None, last=True, rows=256):
    tokens_here = source.shape[0]
    depth = source.shape[1] // 2
    width = pieces[0].shape[1]
    count = len(pieces)
    kind = jnp.bfloat16 if last else jnp.float32

    def row_block(i):
        return (i, 0)

    def whole(i):
        return (0, 0)

    specs = [pl.BlockSpec((rows, depth), lambda i: (i, half))]
    specs += [pl.BlockSpec(p.shape, whole) for p in pieces]
    operands = [source, *pieces]
    out_specs = [pl.BlockSpec((rows, width), row_block)]
    out_shape = [jax.ShapeDtypeStruct((tokens_here, width), kind)]
    if before is not None:
        specs.append(pl.BlockSpec((rows, width), row_block))
        operands.append(before)
    if state is not None:
        specs.append(pl.BlockSpec((width // LANES, rows, LANES), lambda i: (0, i, 0)))
        operands.append(state)
    if edge is not None:
        short, others = edge
        specs += [pl.BlockSpec(a.shape, whole) for a in (short, *others)]
        operands += [short, *others]
        out_specs.append(pl.BlockSpec((short.shape[0], width), whole))
        out_shape.append(jax.ShapeDtypeStruct((short.shape[0], width), kind))
    outs = len(out_shape)

    def kernel(source_ref, *refs):
        weights, extra, out = refs[:count], list(refs[count:-outs]), refs[-outs:]
        total = matmul_sum(source_ref, weights)
        if before is not None:
            total = total + extra.pop(0)[...]
        if state is not None:
            state_ref = extra.pop(0)
            slabs = [state_ref[j] for j in range(width // LANES)]
            total = jax.nn.gelu(total) * jnp.concatenate(slabs, axis=1)
        out[0][...] = total.astype(kind)
        if edge is not None:

            @pl.when(pl.program_id(0) == 0)
            def edge_rows():
                short_ref = extra[0]
                halves = [short_ref.at[:, k * depth : (k + 1) * depth] for k in range(2)]
                ends = matmul_sum(halves[half], weights) + matmul_sum(halves[1 - half], extra[1:])
                out[1][...] = ends.astype(kind)

    return pl.pallas_call(
        kernel,
        grid=(tokens_here // rows,),
        out_shape=out_shape,
        in_specs=specs,
        out_specs=out_specs,
        compiler_params=pltpu.CompilerParams(vmem_limit_bytes=GRANT),
        cost_estimate=pl.CostEstimate(
            flops=2 * tokens_here * depth * width,
            bytes_accessed=2 * (tokens_here * depth + depth * width),
            transcendentals=0,
        ),
        name="project",
    )(*operands)


SUBS = 8
LANES = 128


def advance(decay, drive, cosine, sine, real, imag):
    return (
        decay * (cosine * real - sine * imag) + drive,
        decay * (sine * real + cosine * imag),
    )


def expm1(value):
    near = 1.0 + value * (1.0 / 9.0)
    for k in range(8, 1, -1):
        near = 1.0 + (value * (1.0 / k)) * near
    return jnp.where(value > -0.5, value * near, jnp.exp(value) - 1.0)


def spread_lanes(table_ref, row):
    size = table_ref.shape[1]
    return [
        jnp.broadcast_to(table_ref[row : row + 1, j : j + LANES], (SUBS, LANES))
        for j in range(0, size, LANES)
    ]


def decay_and_drive(convolved, decay_w, input_w, table_ref, taps):
    convolved = convolved.astype(jnp.bfloat16)
    rate = jax.nn.sigmoid(
        jnp.dot(convolved, decay_w[0], preferred_element_type=jnp.float32)
        + table_ref[taps + 1 : taps + 2, :]
    )
    opened = jax.nn.sigmoid(
        jnp.dot(convolved, input_w[0], preferred_element_type=jnp.float32)
        + table_ref[taps + 2 : taps + 3, :]
    )
    log_decay = rate * table_ref[taps + 3 : taps + 4, :]
    drive = jnp.sqrt(-expm1(2.0 * log_decay)) * opened * convolved.astype(jnp.float32)
    return jnp.exp(log_decay), drive


def run_gates(place, x_proj, table, decay_gate, input_gate, taps):
    tokens_here, width = x_proj.shape
    size = decay_gate.shape[1]
    heads = width // size
    length = tokens_here // 2
    part = length // SUBS

    def kernel(
        place_ref, x_ref, table_ref, decay_w, input_w,
        decay_ref, drive_ref, part_ref, total_ref, padded,
    ):
        padded[0:8, :] = jnp.zeros((8, size), jnp.float32)
        padded[8 : 8 + length, :] = x_ref[...].astype(jnp.float32)
        convolved = table_ref[taps : taps + 1, :] + jnp.zeros((length, size), jnp.float32)
        for k in range(taps):
            convolved = convolved + table_ref[k : k + 1, :] * padded[8 - k : 8 - k + length, :]
        decay, drive = decay_and_drive(convolved, decay_w, input_w, table_ref, taps)
        for j in range(size // LANES):
            decay_ref[j] = decay[:, j * LANES : (j + 1) * LANES]
            drive_ref[j] = drive[:, j * LANES : (j + 1) * LANES]
            decay_ref[j, 0 : taps - 1, :] = jnp.ones((taps - 1, LANES), jnp.float32)
            drive_ref[j, 0 : taps - 1, :] = jnp.zeros((taps - 1, LANES), jnp.float32)
        cosines = spread_lanes(table_ref, taps + 4)
        sines = spread_lanes(table_ref, taps + 5)

        def step(t, carry):
            after = []
            for j, (real, imag, product) in enumerate(carry):
                here = decay_ref[j, pl.ds(t, SUBS, stride=part), :]
                push = drive_ref[j, pl.ds(t, SUBS, stride=part), :]
                real, imag = advance(here, push, cosines[j], sines[j], real, imag)
                after.append((real, imag, product * here))
            return tuple(after)

        zeros = jnp.zeros((SUBS, LANES), jnp.float32)
        ends = lax.fori_loop(
            0, part, step, ((zeros, zeros, zeros + 1.0),) * (size // LANES), unroll=8
        )
        real, imag, product = (jnp.concatenate(rows, axis=1) for rows in zip(*ends))
        part_ref[0, 0:SUBS, :] = real
        part_ref[0, SUBS : 2 * SUBS, :] = imag
        part_ref[0, 2 * SUBS : 3 * SUBS, :] = product
        turn_cos, turn_sin = table_ref[taps + 6 : taps + 7, :], table_ref[taps + 7 : taps + 8, :]
        end_real, end_imag = real[0:1], imag[0:1]
        whole = product[0:1]
        for j in range(1, SUBS):
            here = product[j : j + 1]
            end_real, end_imag = (
                here * (turn_cos * end_real - turn_sin * end_imag) + real[j : j + 1],
                here * (turn_sin * end_real + turn_cos * end_imag) + imag[j : j + 1],
            )
            whole = whole * here
        total_ref[0, 0:1, :] = end_real
        total_ref[0, 1:2, :] = end_imag
        total_ref[0, 2:3, :] = whole
        total_ref[0, 3:8, :] = padded[8:13, :]
        total_ref[0, 8:16, :] = padded[length : length + 8, :]

    depth = table.shape[0]
    grid_spec = pltpu.PrefetchScalarGridSpec(
        num_scalar_prefetch=1,
        grid=(heads, 2),
        in_specs=[
            pl.BlockSpec((length, size), lambda h, r, p: (r, h)),
            pl.BlockSpec((depth, size), lambda h, r, p: (0, p[4] * heads + h)),
            pl.BlockSpec((1, size, size), lambda h, r, p: (p[4] * heads + h, 0, 0)),
            pl.BlockSpec((1, size, size), lambda h, r, p: (p[4] * heads + h, 0, 0)),
        ],
        out_specs=[
            pl.BlockSpec((size // LANES, length, LANES), lambda h, r, p: (h, r, 0)),
            pl.BlockSpec((size // LANES, length, LANES), lambda h, r, p: (h, r, 0)),
            pl.BlockSpec((1, 3 * SUBS, size), lambda h, r, p: (r, 0, h)),
            pl.BlockSpec((1, 16, size), lambda h, r, p: (r, 0, h)),
        ],
        scratch_shapes=[pltpu.VMEM((length + 8, size), jnp.float32)],
    )
    return pl.pallas_call(
        kernel,
        grid_spec=grid_spec,
        out_shape=[
            jax.ShapeDtypeStruct((width // LANES, tokens_here, LANES), jnp.float32),
            jax.ShapeDtypeStruct((width // LANES, tokens_here, LANES), jnp.float32),
            jax.ShapeDtypeStruct((2, 3 * SUBS, width), jnp.float32),
            jax.ShapeDtypeStruct((2, 16, width), jnp.float32),
        ],
        compiler_params=pltpu.CompilerParams(vmem_limit_bytes=GRANT),
        cost_estimate=pl.CostEstimate(
            flops=4 * tokens_here * width * size,
            bytes_accessed=10 * tokens_here * width,
            transcendentals=8 * tokens_here * width,
        ),
        name="gates",
    )(place, x_proj, table, decay_gate, input_gate)


def run_states(
    place, decay, drive, parts, totals, table, decay_gate, input_gate, taps, outer, highs
):
    tokens_here, width = decay.shape[1], decay.shape[0] * LANES
    size = decay_gate.shape[1]
    heads = width // size
    length = tokens_here // 2
    part = length // SUBS
    first = taps - 1
    runs = outer * 2 * highs

    def kernel(
        place_ref, decay_ref, drive_ref, part_ref, total_ref, table_ref, decay_w, input_w,
        state_ref, starts, begin, rows_ref, early_decay, early_drive,
    ):
        x, high = place_ref[3], place_ref[5]
        run = pl.program_id(1)

        def row(k):
            return table_ref[taps + k : taps + k + 1, :]

        def turned(here, cosine, sine, real, imag, add_real, add_imag):
            return (
                here * (cosine * real - sine * imag) + add_real,
                here * (sine * real + cosine * imag) + add_imag,
            )

        def begun(base, real, imag):
            here, push = early_decay[pl.ds(base, 8), :], early_drive[pl.ds(base, 8), :]
            for t in range(first):
                real, imag = turned(
                    here[t : t + 1], row(4), row(5), real, imag, push[t : t + 1], 0.0
                )
            return real, imag

        def slot(q):
            at_x, at_run, at_high = q // (2 * highs), q // highs % 2, q % highs
            return ((x ^ at_x) * highs + (high ^ at_high)) * 2 + at_run

        @pl.when(run == 0)
        def every_run():
            zeros = jnp.zeros((8, size), jnp.float32)
            for q in range(runs):
                mine = total_ref[slot(q)]
                if q == 0:
                    rows_ref[0:8, :] = zeros
                else:
                    rows_ref[0:8, :] = total_ref[slot(q - 1)][8:16]
                rows_ref[8:16, :] = zeros
                rows_ref[8 : 8 + first, :] = mine[3 : 3 + first]
                convolved = row(0) + zeros
                for k in range(taps):
                    convolved = convolved + table_ref[k : k + 1, :] * rows_ref[8 - k : 16 - k, :]
                early_drive[q * 8 : q * 8 + 8, :] = convolved
            here, push = decay_and_drive(early_drive[...], decay_w, input_w, table_ref, taps)
            early_decay[...] = here
            early_drive[...] = push
            real = jnp.zeros((1, size), jnp.float32)
            imag = jnp.zeros((1, size), jnp.float32)
            for q in range(runs):
                at_run = q // highs % 2
                ours = (x == q // (2 * highs)) & (high == q % highs)

                @pl.when(ours)
                def keep():
                    begin[8 * at_run : 8 * at_run + 1, :] = real
                    begin[8 * at_run + 1 : 8 * at_run + 2, :] = imag

                if q < runs - 1:
                    mine = total_ref[slot(q)]
                    real, imag = begun(q * 8, real, imag)
                    real, imag = turned(
                        mine[2:3], row(8), row(9), real, imag, mine[0:1], mine[1:2]
                    )

        base = pl.multiple_of(((x * 2 + run) * highs + high) * 8, 8)
        kept = begin[pl.ds(pl.multiple_of(run * 8, 8), 8), :]
        real, imag = kept[0:1], kept[1:2]
        early_here, early_push = early_decay[pl.ds(base, 8), :], early_drive[pl.ds(base, 8), :]
        for j in range(SUBS):
            starts[j : j + 1, :] = real
            starts[SUBS + j : SUBS + j + 1, :] = imag
            if j == 0:
                real, imag = begun(base, real, imag)
            spin = row(10), row(11)
            if j > 0:
                spin = row(6), row(7)
            real, imag = turned(
                part_ref[0, 2 * SUBS + j : 2 * SUBS + j + 1, :], *spin, real, imag,
                part_ref[0, j : j + 1, :], part_ref[0, SUBS + j : SUBS + j + 1, :],
            )
        cosines = spread_lanes(table_ref, taps + 4)
        sines = spread_lanes(table_ref, taps + 5)
        top = lax.broadcasted_iota(jnp.int32, (SUBS, LANES), 0) == 0

        def step(t, carry, early=False):
            after = []
            for j, (real, imag) in enumerate(carry):
                here = decay_ref[j, pl.ds(t, SUBS, stride=part), :]
                push = drive_ref[j, pl.ds(t, SUBS, stride=part), :]
                if early:
                    lanes = slice(j * LANES, (j + 1) * LANES)
                    here = jnp.where(top, early_here[t : t + 1, lanes], here)
                    push = jnp.where(top, early_push[t : t + 1, lanes], push)
                real, imag = advance(here, push, cosines[j], sines[j], real, imag)
                state_ref[j, pl.ds(t, SUBS, stride=part), :] = real
                after.append((real, imag))
            return tuple(after)

        carry = tuple(
            (starts[0:SUBS, j : j + LANES], starts[SUBS : 2 * SUBS, j : j + LANES])
            for j in range(0, size, LANES)
        )
        for t in range(8):
            carry = step(t, carry, t < first)
        lax.fori_loop(8, part, step, carry, unroll=8)

    depth = table.shape[0]
    slots = totals.shape[0]
    grid_spec = pltpu.PrefetchScalarGridSpec(
        num_scalar_prefetch=1,
        grid=(heads, 2),
        in_specs=[
            pl.BlockSpec((size // LANES, length, LANES), lambda h, r, p: (h, r, 0)),
            pl.BlockSpec((size // LANES, length, LANES), lambda h, r, p: (h, r, 0)),
            pl.BlockSpec((1, 3 * SUBS, size), lambda h, r, p: (r, 0, h)),
            pl.BlockSpec((slots, 16, size), lambda h, r, p: (0, 0, h)),
            pl.BlockSpec((depth, size), lambda h, r, p: (0, p[4] * heads + h)),
            pl.BlockSpec((1, size, size), lambda h, r, p: (p[4] * heads + h, 0, 0)),
            pl.BlockSpec((1, size, size), lambda h, r, p: (p[4] * heads + h, 0, 0)),
        ],
        out_specs=pl.BlockSpec((size // LANES, length, LANES), lambda h, r, p: (h, r, 0)),
        scratch_shapes=[
            pltpu.VMEM((2 * SUBS, size), jnp.float32),
            pltpu.VMEM((16, size), jnp.float32),
            pltpu.VMEM((16, size), jnp.float32),
            pltpu.VMEM((runs * 8, size), jnp.float32),
            pltpu.VMEM((runs * 8, size), jnp.float32),
        ],
    )
    return pl.pallas_call(
        kernel,
        grid_spec=grid_spec,
        out_shape=jax.ShapeDtypeStruct((width // LANES, tokens_here, LANES), jnp.float32),
        compiler_params=pltpu.CompilerParams(vmem_limit_bytes=GRANT),
        cost_estimate=pl.CostEstimate(
            flops=10 * tokens_here * width,
            bytes_accessed=12 * tokens_here * width,
            transcendentals=0,
        ),
        name="states",
    )(place, decay, drive, parts, totals, table, decay_gate, input_gate)


def products(c, gated, weights):
    deep = gated[0].shape[1]
    spots = [pl.multiple_of((c ^ e) * deep, deep) for e in range(2)]
    blocks = []
    for weight in weights:
        terms = [
            jnp.dot(
                gated[e][...], weight[pl.ds(spots[e], deep), :], preferred_element_type=jnp.float32
            )
            for e in range(2)
        ]
        blocks.append(terms[0] + terms[1])
    return blocks


def mix_near(place, parts, pieces):
    tokens_here, deep = parts[0].shape
    width = pieces[0].shape[1]
    rows = tokens_here // 4
    count = len(pieces)

    def kernel(place_ref, *refs):
        blocks = products(place_ref[0], refs[:2], refs[2:-1])
        for b in range(count):
            refs[-1][:, b * width : (b + 1) * width] = blocks[b]

    return pl.pallas_call(
        kernel,
        grid=(4,),
        out_shape=jax.ShapeDtypeStruct((tokens_here, count * width), jnp.float32),
        in_specs=[SMEM]
        + [pl.BlockSpec((rows, deep), lambda i: (i, 0))] * 2
        + [pl.BlockSpec(piece.shape, lambda i: (0, 0)) for piece in pieces],
        out_specs=pl.BlockSpec((rows, count * width), lambda i: (i, 0)),
        compiler_params=pltpu.CompilerParams(vmem_limit_bytes=GRANT),
        cost_estimate=pl.CostEstimate(
            flops=4 * count * tokens_here * deep * width,
            bytes_accessed=4 * tokens_here * deep + 16 * count * rows * width,
            transcendentals=0,
        ),
        name="mix_near",
    )(place, *parts, *pieces)


def mix_far(place, parts, pieces, near):
    tokens_here, deep = parts[0].shape
    width = pieces[0].shape[1]
    rows = tokens_here // 4
    count = len(pieces)
    parts = [value.reshape(2, 2, rows, deep) for value in parts]
    near = near.reshape(2, 2, rows, count * width)

    def kernel(place_ref, *refs):
        near_ref, leaves, stays = refs[-5], refs[-4:-2], refs[-2:]
        c = place_ref[0]
        gated = [ref[...].reshape(2 * rows, deep) for ref in refs[:2]]
        blocks = products(c, gated, refs[2:-5])
        sums = near_ref[...].reshape(2 * rows, count * width)
        blocks = [block + sums[:, b * width : (b + 1) * width] for b, block in enumerate(blocks)]

        def write(targets, order):
            for at_c in range(2):

                @pl.when(c == at_c)
                def write_runs():
                    for e, target in enumerate(targets):
                        run = at_c ^ e
                        for b in range(count):
                            at = order(b) * width
                            target[:, at : at + width] = blocks[b][
                                run * rows : (run + 1) * rows
                            ].astype(target.dtype)

        @pl.when(pl.program_id(0) == 0)
        def leave():
            write(leaves, lambda b: count - 1 - b)

        @pl.when(pl.program_id(0) == 1)
        def stay():
            write(stays, lambda b: b)

    def lows(f, p):
        return (0, 1 - f ^ p[6], 0, 0)

    grid_spec = pltpu.PrefetchScalarGridSpec(
        num_scalar_prefetch=1,
        grid=(2,),
        in_specs=[pl.BlockSpec((2, 1, rows, deep), lows) for _ in parts]
        + [pl.BlockSpec(piece.shape, lambda f, p: (0, 0)) for piece in pieces]
        + [pl.BlockSpec((2, 1, rows, count * width), lows)],
        out_specs=[pl.BlockSpec((rows, count * width), lambda f, p: (0, 0))] * 4,
    )
    kinds = [jnp.bfloat16, jnp.bfloat16, jnp.float32, jnp.bfloat16]
    return pl.pallas_call(
        kernel,
        grid_spec=grid_spec,
        out_shape=[jax.ShapeDtypeStruct((rows, count * width), kind) for kind in kinds],
        compiler_params=pltpu.CompilerParams(vmem_limit_bytes=GRANT),
        cost_estimate=pl.CostEstimate(
            flops=4 * count * tokens_here * deep * width,
            bytes_accessed=4 * tokens_here * deep + 28 * count * rows * width,
            transcendentals=0,
        ),
        name="mix_far",
    )(place, *parts, *pieces, near)


def place_columns(place, groups, terms, block):
    rows = terms[0].shape[0]
    segs = sum(len(group) for group in groups)

    def kernel(place_ref, *refs):
        c, z = place_ref[0], place_ref[1]
        whole = refs[-1]
        for i, group in enumerate(groups):
            for j, b in enumerate(group):
                for d in range(2):
                    at = pl.multiple_of(((c ^ d) * segs + (z ^ b)) * block, block)
                    one, two = (
                        ref[:, j * block : (j + 1) * block].astype(jnp.float32)
                        for ref in refs[4 * i + 2 * d : 4 * i + 2 * d + 2]
                    )
                    whole[:, pl.ds(at, block)] = (one + two).astype(whole.dtype)

    return pl.pallas_call(
        kernel,
        out_shape=jax.ShapeDtypeStruct((rows, 2 * segs * block), jnp.bfloat16),
        in_specs=[SMEM] + [VMEM] * len(terms),
        out_specs=VMEM,
        name="place",
    )(place, *terms)


def folded(
    tokens,
    x_weight,
    y_weight,
    out_weight,
    conv_weight,
    conv_bias,
    decay_gate,
    decay_bias,
    input_gate,
    input_bias,
    log_rate,
    phase,
):
    grps, segs = lax.axis_size("grp"), lax.axis_size("seg")
    g, z, y = lax.axis_index("grp"), lax.axis_index("seg"), lax.axis_index("mp")
    outer, highs = grps // 2, segs // 2
    x, c = g // 2, g % 2
    high, low = z // 2, z % 2
    turn = x ^ y
    rows, _ = tokens.shape
    columns = x_weight.shape[1]
    width = columns // 4
    taps = conv_weight.shape[0]
    length = 2 * rows
    place = jnp.stack([c, z, turn, x, low * 2 + c, high, low]).astype(jnp.int32)

    part = length // SUBS

    def less(count):
        c_all, s_all = jnp.cos(count * phase), jnp.sin(count * phase)
        c_few, s_few = jnp.cos((taps - 1) * phase), jnp.sin((taps - 1) * phase)
        return c_all * c_few + s_all * s_few, s_all * c_few - c_all * s_few

    table = jnp.stack(
        [conv_weight[k] for k in range(taps)]
        + [
            conv_bias,
            decay_bias,
            input_bias,
            -8.0 * jax.nn.softplus(log_rate),
            jnp.cos(phase),
            jnp.sin(phase),
            jnp.cos(part * phase),
            jnp.sin(part * phase),
            *less(length),
            *less(part),
        ]
    )

    by_z = swap(tokens, "seg", 1)
    here = [tokens, swap(tokens, "mp", 1), by_z, swap(by_z, "mp", 1)]
    tied, table = lax.optimization_barrier((tokens, table))
    there = [swap(piece, "grp", 1) for piece in [tied] + here[1:]]

    source = assemble(place, here + there, segs)

    def cut(weight, at_low, at_c):
        return lax.dynamic_slice(
            weight, (0, at_low * (2 * width) + at_c * width), (weight.shape[0], width)
        )

    def columns_of(weight):
        leaving = jnp.concatenate([cut(weight, low, 1 - c), cut(weight, 1 - low, 1 - c)])
        arrived = swap(leaving, "grp", 1)
        deep = weight.shape[0]
        own = jnp.concatenate([cut(weight, low, c), arrived[:deep]])
        other = jnp.concatenate([cut(weight, 1 - low, c), arrived[deep:]])
        return spread(own, other)

    x_near, x_far = columns_of(x_weight)
    y_near, y_far = columns_of(y_weight)

    half = 2 * width
    out_columns = out_weight.shape[1]
    out_near, out_far = spread(
        lax.dynamic_slice(out_weight, (low * half, 0), (half, out_columns)),
        lax.dynamic_slice(out_weight, ((1 - low) * half, 0), (half, out_columns)),
    )
    diagonal = turn == 0
    out_pieces = []
    for mine, theirs in zip(out_near, out_far):
        kept = jnp.where(diagonal, mine, theirs)
        passed = jnp.where(diagonal, theirs, mine)
        out_pieces.append((kept, swap(passed, "mp", 1)))

    (x_part,) = project(source, 0, x_near, last=False)
    (x_proj,) = project(source, 1, x_far, before=x_part)
    (y_part,) = project(source, 0, y_near, last=False)

    decay, drive, parts, total = run_gates(
        place, x_proj, table, decay_gate, input_gate, taps
    )
    totals = [total] + [swap(total, "seg", 2 * j) for j in range(1, highs)]
    totals = jnp.stack(totals)
    totals = [totals] + [swap(totals, "grp", 2 * i) for i in range(1, outer)]
    totals = jnp.stack(totals).reshape(outer * highs * 2, *total.shape[1:])
    state = run_states(
        place, decay, drive, parts, totals, table, decay_gate, input_gate, taps, outer, highs
    )

    (gated,) = project(source, 1, y_far, before=y_part, state=state)
    gated_y = swap(gated, "mp", 1)
    gated_near = [gated, swap(gated, "grp", 1)]
    gated_far = [gated_y, swap(gated_y, "grp", 1)]
    groups = [(b, b + 1) for b in range(0, segs - 2, 2)] + [(segs - 2,), (segs - 1,)]
    nears = []
    for group in groups:
        nears.append(mix_near(place, gated_near, [out_pieces[b][0] for b in group]))

    crossed = [
        (og * segs + oz, (og ^ 1) * segs + (oz ^ 1)) for og in range(grps) for oz in range(segs)
    ]
    kept, arrived = [], {}
    for group, near in zip(groups, nears):
        name = group[0]
        pieces = [out_pieces[b][1] for b in group]
        leave, leave_far, stay, stay_far = mix_far(place, gated_far, pieces, near)
        kept.append((stay, swap(stay_far, "grp", 1)))
        over = lax.ppermute(leave_far, ("grp", "seg"), crossed)
        partner = name if len(group) == 2 else name ^ 1
        arrived[partner] = (swap(leave, "seg", 1), over)
    terms = []
    for group, (stay, stay_far) in zip(groups, kept):
        leave, leave_far = arrived[group[0]]
        terms += [stay, leave, stay_far, leave_far]
    return place_columns(place, groups, terms, out_columns)


def solution(mesh):
    grps, segs, mps = mesh.shape["grp"], mesh.shape["seg"], mesh.shape["mp"]
    powers = segs >= 4 and segs & (segs - 1) == 0
    fits = grps == 2 * mps and mps == 2 and powers
    in_specs = (
        P(("grp", "seg"), "mp"),
        P(("grp", "seg"), "mp"),
        P(("grp", "seg"), "mp"),
        P("mp", ("grp", "seg")),
        P(None, "mp"),
        P("mp"),
        P("mp", None, None),
        P("mp"),
        P("mp", None, None),
        P("mp"),
        P("mp"),
        P("mp"),
    )
    out_specs = P(("grp", "seg"), "mp")

    def local(*arrays):
        return (folded if fits else general)(*arrays)

    return jax.shard_map(local, mesh=mesh, in_specs=in_specs, out_specs=out_specs, check_vma=False)
```

```python
import jax
import jax.numpy as jnp
from jax import lax
from jax.experimental import pallas as pl
from jax.experimental.pallas import tpu as pltpu
from jax.sharding import PartitionSpec as P


VMEM = pl.BlockSpec(memory_space=pltpu.VMEM)
SMEM = pl.BlockSpec(memory_space=pltpu.SMEM)
GRANT = 56 * 1024 * 1024


def shifted(value, axis, by):
    peers = lax.axis_size(axis)
    pairs = [(i, i + by) for i in range(peers) if 0 <= i + by < peers]
    return lax.ppermute(value, axis, pairs)


def carried_in(value, axis, join, neutral):
    count, mine = (lax.axis_size(axis), lax.axis_index(axis))
    pieces = lax.all_gather(value, axis)
    total = jnp.full_like(value, 0) + jnp.asarray(neutral, value.dtype)

    def turn(position, total):
        longer = join(total, pieces[position])
        return jnp.where(position < mine, longer, total)

    return lax.fori_loop(0, count - 1, turn, total)


def combine(earlier, later):
    first_real = earlier[0] * later[0] - earlier[1] * later[1]
    first_imag = earlier[0] * later[1] + earlier[1] * later[0]
    state_real = later[0] * earlier[2] - later[1] * earlier[3] + later[2]
    state_imag = later[0] * earlier[3] + later[1] * earlier[2] + later[3]
    return jnp.stack([first_real, first_imag, state_real, state_imag])


def neutral(count):
    ones_row = jnp.ones((count,), jnp.float32)
    zeros_row = jnp.zeros((count,), jnp.float32)
    return jnp.stack([ones_row, zeros_row, zeros_row, zeros_row])


def general(
    tokens,
    x_weight,
    y_weight,
    out_weight,
    conv_weight,
    conv_bias,
    decay_gate,
    decay_bias,
    input_gate,
    input_bias,
    log_rate,
    phase,
):
    source = lax.all_gather(tokens, "mp", axis=1, tiled=True)
    tokens_here = source.shape[0]
    width = x_weight.shape[1]

    def add_rows(shard_piece):
        return jnp.dot(source, shard_piece, preferred_element_type=jnp.float32)

    x_sum = add_rows(lax.all_gather(x_weight, ("grp", "seg"), axis=0, tiled=True))
    y_sum = add_rows(lax.all_gather(y_weight, ("grp", "seg"), axis=0, tiled=True))
    x_proj = x_sum.astype(jnp.bfloat16)
    branch = jax.nn.gelu(y_sum)
    taps = conv_weight.shape[0]
    last_rows = x_proj[tokens_here - (taps - 1) :]
    before = shifted(last_rows, ("grp", "seg"), 1)
    padded = jnp.concatenate([before, x_proj], axis=0).astype(jnp.float32)
    convolved = conv_bias + jnp.zeros((tokens_here, width), jnp.float32)
    for offset in range(taps):
        convolved = (
            convolved
            + conv_weight[offset] * padded[taps - 1 - offset : taps - 1 - offset + tokens_here]
        )
    convolved = convolved.astype(jnp.bfloat16)
    heads_here = decay_gate.shape[0]
    block_size = decay_gate.shape[1]
    head_view = convolved.reshape(tokens_here, heads_here, block_size)
    rate_gate = jax.nn.sigmoid(
        jnp.einsum(
            "nhd,hde->nhe", head_view, decay_gate, preferred_element_type=jnp.float32
        ).reshape(tokens_here, width)
        + decay_bias
    )
    input_open = jax.nn.sigmoid(
        jnp.einsum(
            "nhd,hde->nhe", head_view, input_gate, preferred_element_type=jnp.float32
        ).reshape(tokens_here, width)
        + input_bias
    )
    log_decay = -8.0 * rate_gate * jax.nn.softplus(log_rate)
    decay = jnp.exp(log_decay)
    drive = jnp.sqrt(-jnp.expm1(2.0 * log_decay)) * input_open * convolved.astype(jnp.float32)
    elements = jnp.stack(
        [decay * jnp.cos(phase), decay * jnp.sin(phase), drive, jnp.zeros_like(drive)]
    )
    running = lax.associative_scan(combine, elements, axis=1)
    summary = running[:, tokens_here - 1]
    identity = neutral(width)
    carry_in = carried_in(summary, ("grp", "seg"), combine, identity)
    state_real = running[2] + running[0] * carry_in[2] - running[1] * carry_in[3]
    gated = (branch * state_real).astype(jnp.bfloat16)
    partial_value = jnp.dot(
        gated,
        lax.all_gather(out_weight, ("grp", "seg"), axis=1, tiled=True),
        preferred_element_type=jnp.float32,
    )
    reduced = lax.psum_scatter(
        partial_value.astype(jnp.bfloat16), "mp", scatter_dimension=1, tiled=True
    )
    return reduced


def swap(value, axis, bit):
    count = lax.axis_size(axis)
    return lax.ppermute(value, axis, [(i, i ^ bit) for i in range(count)])


def spread(own, other):
    near = [own]
    for b in range(1, lax.axis_size("seg")):
        near.append(swap(other if b % 2 else own, "seg", b))
    return near, [swap(piece, "grp", 2) for piece in near]


def assemble(place, pieces, segs):
    rows, wide = pieces[0].shape
    lows = len(pieces) // 4
    block = wide // 2 // segs

    def kernel(place_ref, *refs):
        c, z, turn, low = place_ref[0], place_ref[1], place_ref[2], place_ref[6]
        for b in range(segs):
            for d in range(2):
                source = pl.multiple_of(((c ^ d) * segs + (z ^ b)) * block, block)
                for index, piece in enumerate(refs[:-1]):
                    e, f, h = index // (2 * lows), index // 2 % lows, index % 2
                    at_low = low ^ f if lows == 2 else 0
                    row = pl.multiple_of(((c ^ e) * lows + at_low) * rows, rows)
                    column = pl.multiple_of((turn ^ h) * wide + (b * 2 + d) * block, block)
                    refs[-1][pl.ds(row, rows), pl.ds(column, block)] = piece[
                        :, pl.ds(source, block)
                    ]

    return pl.pallas_call(
        kernel,
        out_shape=jax.ShapeDtypeStruct((2 * lows * rows, 2 * wide), pieces[0].dtype),
        in_specs=[SMEM] + [VMEM] * len(pieces),
        out_specs=VMEM,
        compiler_params=pltpu.CompilerParams(vmem_limit_bytes=GRANT),
        cost_estimate=pl.CostEstimate(
            flops=0, bytes_accessed=4 * len(pieces) * rows * wide, transcendentals=0
        ),
        name="set_together",
    )(place, *pieces)


def matmul_sum(source, pieces):
    deep = pieces[0].shape[0]
    total = None
    for index, piece in enumerate(pieces):
        term = jnp.dot(
            source[:, index * deep : (index + 1) * deep],
            piece[...],
            preferred_element_type=jnp.float32,
        )
        total = term if total is None else total + term
    return total


def project(source, half, pieces, edge=None, before=None, state=None, last=True, rows=512):
    tokens_here = source.shape[0]
    depth = source.shape[1] // 2
    width = pieces[0].shape[1]
    count = len(pieces)
    kind = jnp.bfloat16 if last else jnp.float32

    def row_block(i):
        return (i, 0)

    def whole(i):
        return (0, 0)

    specs = [pl.BlockSpec((rows, depth), lambda i: (i, half))]
    specs += [pl.BlockSpec(p.shape, whole) for p in pieces]
    operands = [source, *pieces]
    out_specs = [pl.BlockSpec((rows, width), row_block)]
    out_shape = [jax.ShapeDtypeStruct((tokens_here, width), kind)]
    if before is not None:
        specs.append(pl.BlockSpec((rows, width), row_block))
        operands.append(before)
    if state is not None:
        specs.append(pl.BlockSpec((width // LANES, rows, LANES), lambda i: (0, i, 0)))
        operands.append(state)
    if edge is not None:
        short, others = edge
        specs += [pl.BlockSpec(a.shape, whole) for a in (short, *others)]
        operands += [short, *others]
        out_specs.append(pl.BlockSpec((short.shape[0], width), whole))
        out_shape.append(jax.ShapeDtypeStruct((short.shape[0], width), kind))
    outs = len(out_shape)

    def kernel(source_ref, *refs):
        weights, extra, out = refs[:count], list(refs[count:-outs]), refs[-outs:]
        total = matmul_sum(source_ref, weights)
        if before is not None:
            total = total + extra.pop(0)[...]
        if state is not None:
            state_ref = extra.pop(0)
            slabs = [state_ref[j] for j in range(width // LANES)]
            total = jax.nn.gelu(total) * jnp.concatenate(slabs, axis=1)
        out[0][...] = total.astype(kind)
        if edge is not None:

            @pl.when(pl.program_id(0) == 0)
            def edge_rows():
                short_ref = extra[0]
                halves = [short_ref.at[:, k * depth : (k + 1) * depth] for k in range(2)]
                ends = matmul_sum(halves[half], weights) + matmul_sum(halves[1 - half], extra[1:])
                out[1][...] = ends.astype(kind)

    return pl.pallas_call(
        kernel,
        grid=(tokens_here // rows,),
        out_shape=out_shape,
        in_specs=specs,
        out_specs=out_specs,
        compiler_params=pltpu.CompilerParams(vmem_limit_bytes=GRANT),
        cost_estimate=pl.CostEstimate(
            flops=2 * tokens_here * depth * width,
            bytes_accessed=2 * (tokens_here * depth + depth * width),
            transcendentals=0,
        ),
        name="project",
    )(*operands)


SUBS = 8
LANES = 128


def advance(decay, drive, cosine, sine, real, imag):
    return (
        decay * (cosine * real - sine * imag) + drive,
        decay * (sine * real + cosine * imag),
    )


def expm1(value):
    near = 1.0 + value * (1.0 / 9.0)
    for k in range(8, 1, -1):
        near = 1.0 + (value * (1.0 / k)) * near
    return jnp.where(value > -0.5, value * near, jnp.exp(value) - 1.0)


def spread_lanes(table_ref, row):
    size = table_ref.shape[1]
    return [
        jnp.broadcast_to(table_ref[row : row + 1, j : j + LANES], (SUBS, LANES))
        for j in range(0, size, LANES)
    ]


def decay_and_drive(convolved, decay_w, input_w, table_ref, taps):
    convolved = convolved.astype(jnp.bfloat16)
    rate = jax.nn.sigmoid(
        jnp.dot(convolved, decay_w[0], preferred_element_type=jnp.float32)
        + table_ref[taps + 1 : taps + 2, :]
    )
    opened = jax.nn.sigmoid(
        jnp.dot(convolved, input_w[0], preferred_element_type=jnp.float32)
        + table_ref[taps + 2 : taps + 3, :]
    )
    log_decay = rate * table_ref[taps + 3 : taps + 4, :]
    drive = jnp.sqrt(-expm1(2.0 * log_decay)) * opened * convolved.astype(jnp.float32)
    return jnp.exp(log_decay), drive


def run_gates(place, x_proj, table, decay_gate, input_gate, taps):
    tokens_here, width = x_proj.shape
    size = decay_gate.shape[1]
    heads = width // size
    length = tokens_here // 2
    part = length // SUBS

    def kernel(
        place_ref, x_ref, table_ref, decay_w, input_w,
        decay_ref, drive_ref, part_ref, total_ref, padded,
    ):
        padded[0:8, :] = jnp.zeros((8, size), jnp.float32)
        padded[8 : 8 + length, :] = x_ref[...].astype(jnp.float32)
        convolved = table_ref[taps : taps + 1, :] + jnp.zeros((length, size), jnp.float32)
        for k in range(taps):
            convolved = convolved + table_ref[k : k + 1, :] * padded[8 - k : 8 - k + length, :]
        decay, drive = decay_and_drive(convolved, decay_w, input_w, table_ref, taps)
        for j in range(size // LANES):
            decay_ref[j] = decay[:, j * LANES : (j + 1) * LANES]
            drive_ref[j] = drive[:, j * LANES : (j + 1) * LANES]
            decay_ref[j, 0 : taps - 1, :] = jnp.ones((taps - 1, LANES), jnp.float32)
            drive_ref[j, 0 : taps - 1, :] = jnp.zeros((taps - 1, LANES), jnp.float32)
        cosines = spread_lanes(table_ref, taps + 4)
        sines = spread_lanes(table_ref, taps + 5)

        def step(t, carry):
            after = []
            for j, (real, imag, product) in enumerate(carry):
                here = decay_ref[j, pl.ds(t, SUBS, stride=part), :]
                push = drive_ref[j, pl.ds(t, SUBS, stride=part), :]
                real, imag = advance(here, push, cosines[j], sines[j], real, imag)
                after.append((real, imag, product * here))
            return tuple(after)

        zeros = jnp.zeros((SUBS, LANES), jnp.float32)
        ends = lax.fori_loop(
            0, part, step, ((zeros, zeros, zeros + 1.0),) * (size // LANES), unroll=8
        )
        real, imag, product = (jnp.concatenate(rows, axis=1) for rows in zip(*ends))
        part_ref[0, 0:SUBS, :] = real
        part_ref[0, SUBS : 2 * SUBS, :] = imag
        part_ref[0, 2 * SUBS : 3 * SUBS, :] = product
        turn_cos, turn_sin = table_ref[taps + 6 : taps + 7, :], table_ref[taps + 7 : taps + 8, :]
        end_real, end_imag = real[0:1], imag[0:1]
        whole = product[0:1]
        for j in range(1, SUBS):
            here = product[j : j + 1]
            end_real, end_imag = (
                here * (turn_cos * end_real - turn_sin * end_imag) + real[j : j + 1],
                here * (turn_sin * end_real + turn_cos * end_imag) + imag[j : j + 1],
            )
            whole = whole * here
        total_ref[0, 0:1, :] = end_real
        total_ref[0, 1:2, :] = end_imag
        total_ref[0, 2:3, :] = whole
        total_ref[0, 3:8, :] = padded[8:13, :]
        total_ref[0, 8:16, :] = padded[length : length + 8, :]

    depth = table.shape[0]
    grid_spec = pltpu.PrefetchScalarGridSpec(
        num_scalar_prefetch=1,
        grid=(heads, 2),
        in_specs=[
            pl.BlockSpec((length, size), lambda h, r, p: (r, h)),
            pl.BlockSpec((depth, size), lambda h, r, p: (0, p[4] * heads + h)),
            pl.BlockSpec((1, size, size), lambda h, r, p: (p[4] * heads + h, 0, 0)),
            pl.BlockSpec((1, size, size), lambda h, r, p: (p[4] * heads + h, 0, 0)),
        ],
        out_specs=[
            pl.BlockSpec((size // LANES, length, LANES), lambda h, r, p: (h, r, 0)),
            pl.BlockSpec((size // LANES, length, LANES), lambda h, r, p: (h, r, 0)),
            pl.BlockSpec((1, 3 * SUBS, size), lambda h, r, p: (r, 0, h)),
            pl.BlockSpec((1, 16, size), lambda h, r, p: (r, 0, h)),
        ],
        scratch_shapes=[pltpu.VMEM((length + 8, size), jnp.float32)],
    )
    return pl.pallas_call(
        kernel,
        grid_spec=grid_spec,
        out_shape=[
            jax.ShapeDtypeStruct((width // LANES, tokens_here, LANES), jnp.float32),
            jax.ShapeDtypeStruct((width // LANES, tokens_here, LANES), jnp.float32),
            jax.ShapeDtypeStruct((2, 3 * SUBS, width), jnp.float32),
            jax.ShapeDtypeStruct((2, 16, width), jnp.float32),
        ],
        compiler_params=pltpu.CompilerParams(vmem_limit_bytes=GRANT),
        cost_estimate=pl.CostEstimate(
            flops=4 * tokens_here * width * size,
            bytes_accessed=10 * tokens_here * width,
            transcendentals=8 * tokens_here * width,
        ),
        name="gates",
    )(place, x_proj, table, decay_gate, input_gate)


def run_states(
    place, decay, drive, parts, totals, table, decay_gate, input_gate, taps, outer, highs
):
    tokens_here, width = decay.shape[1], decay.shape[0] * LANES
    size = decay_gate.shape[1]
    heads = width // size
    length = tokens_here // 2
    part = length // SUBS
    first = taps - 1
    runs = outer * 2 * highs

    def kernel(
        place_ref, decay_ref, drive_ref, part_ref, total_ref, table_ref, decay_w, input_w,
        state_ref, starts, begin, rows_ref, early_decay, early_drive,
    ):
        x, high = place_ref[3], place_ref[5]
        run = pl.program_id(1)

        def row(k):
            return table_ref[taps + k : taps + k + 1, :]

        def turned(here, cosine, sine, real, imag, add_real, add_imag):
            return (
                here * (cosine * real - sine * imag) + add_real,
                here * (sine * real + cosine * imag) + add_imag,
            )

        def begun(base, real, imag):
            here, push = early_decay[pl.ds(base, 8), :], early_drive[pl.ds(base, 8), :]
            for t in range(first):
                real, imag = turned(
                    here[t : t + 1], row(4), row(5), real, imag, push[t : t + 1], 0.0
                )
            return real, imag

        def slot(q):
            at_x, at_run, at_high = q // (2 * highs), q // highs % 2, q % highs
            return ((x ^ at_x) * highs + (high ^ at_high)) * 2 + at_run

        @pl.when(run == 0)
        def every_run():
            zeros = jnp.zeros((8, size), jnp.float32)
            for q in range(runs):
                mine = total_ref[slot(q)]
                if q == 0:
                    rows_ref[0:8, :] = zeros
                else:
                    rows_ref[0:8, :] = total_ref[slot(q - 1)][8:16]
                rows_ref[8:16, :] = zeros
                rows_ref[8 : 8 + first, :] = mine[3 : 3 + first]
                convolved = row(0) + zeros
                for k in range(taps):
                    convolved = convolved + table_ref[k : k + 1, :] * rows_ref[8 - k : 16 - k, :]
                early_drive[q * 8 : q * 8 + 8, :] = convolved
            here, push = decay_and_drive(early_drive[...], decay_w, input_w, table_ref, taps)
            early_decay[...] = here
            early_drive[...] = push
            real = jnp.zeros((1, size), jnp.float32)
            imag = jnp.zeros((1, size), jnp.float32)
            for q in range(runs):
                at_run = q // highs % 2
                ours = (x == q // (2 * highs)) & (high == q % highs)

                @pl.when(ours)
                def keep():
                    begin[8 * at_run : 8 * at_run + 1, :] = real
                    begin[8 * at_run + 1 : 8 * at_run + 2, :] = imag

                if q < runs - 1:
                    mine = total_ref[slot(q)]
                    real, imag = begun(q * 8, real, imag)
                    real, imag = turned(
                        mine[2:3], row(8), row(9), real, imag, mine[0:1], mine[1:2]
                    )

        base = pl.multiple_of(((x * 2 + run) * highs + high) * 8, 8)
        kept = begin[pl.ds(pl.multiple_of(run * 8, 8), 8), :]
        real, imag = kept[0:1], kept[1:2]
        early_here, early_push = early_decay[pl.ds(base, 8), :], early_drive[pl.ds(base, 8), :]
        for j in range(SUBS):
            starts[j : j + 1, :] = real
            starts[SUBS + j : SUBS + j + 1, :] = imag
            if j == 0:
                real, imag = begun(base, real, imag)
            spin = row(10), row(11)
            if j > 0:
                spin = row(6), row(7)
            real, imag = turned(
                part_ref[0, 2 * SUBS + j : 2 * SUBS + j + 1, :], *spin, real, imag,
                part_ref[0, j : j + 1, :], part_ref[0, SUBS + j : SUBS + j + 1, :],
            )
        cosines = spread_lanes(table_ref, taps + 4)
        sines = spread_lanes(table_ref, taps + 5)
        top = lax.broadcasted_iota(jnp.int32, (SUBS, LANES), 0) == 0

        def step(t, carry, early=False):
            after = []
            for j, (real, imag) in enumerate(carry):
                here = decay_ref[j, pl.ds(t, SUBS, stride=part), :]
                push = drive_ref[j, pl.ds(t, SUBS, stride=part), :]
                if early:
                    lanes = slice(j * LANES, (j + 1) * LANES)
                    here = jnp.where(top, early_here[t : t + 1, lanes], here)
                    push = jnp.where(top, early_push[t : t + 1, lanes], push)
                real, imag = advance(here, push, cosines[j], sines[j], real, imag)
                state_ref[j, pl.ds(t, SUBS, stride=part), :] = real
                after.append((real, imag))
            return tuple(after)

        carry = tuple(
            (starts[0:SUBS, j : j + LANES], starts[SUBS : 2 * SUBS, j : j + LANES])
            for j in range(0, size, LANES)
        )
        for t in range(8):
            carry = step(t, carry, t < first)
        lax.fori_loop(8, part, step, carry, unroll=8)

    depth = table.shape[0]
    slots = totals.shape[0]
    grid_spec = pltpu.PrefetchScalarGridSpec(
        num_scalar_prefetch=1,
        grid=(heads, 2),
        in_specs=[
            pl.BlockSpec((size // LANES, length, LANES), lambda h, r, p: (h, r, 0)),
            pl.BlockSpec((size // LANES, length, LANES), lambda h, r, p: (h, r, 0)),
            pl.BlockSpec((1, 3 * SUBS, size), lambda h, r, p: (r, 0, h)),
            pl.BlockSpec((slots, 16, size), lambda h, r, p: (0, 0, h)),
            pl.BlockSpec((depth, size), lambda h, r, p: (0, p[4] * heads + h)),
            pl.BlockSpec((1, size, size), lambda h, r, p: (p[4] * heads + h, 0, 0)),
            pl.BlockSpec((1, size, size), lambda h, r, p: (p[4] * heads + h, 0, 0)),
        ],
        out_specs=pl.BlockSpec((size // LANES, length, LANES), lambda h, r, p: (h, r, 0)),
        scratch_shapes=[
            pltpu.VMEM((2 * SUBS, size), jnp.float32),
            pltpu.VMEM((16, size), jnp.float32),
            pltpu.VMEM((16, size), jnp.float32),
            pltpu.VMEM((runs * 8, size), jnp.float32),
            pltpu.VMEM((runs * 8, size), jnp.float32),
        ],
    )
    return pl.pallas_call(
        kernel,
        grid_spec=grid_spec,
        out_shape=jax.ShapeDtypeStruct((width // LANES, tokens_here, LANES), jnp.float32),
        compiler_params=pltpu.CompilerParams(vmem_limit_bytes=GRANT),
        cost_estimate=pl.CostEstimate(
            flops=10 * tokens_here * width,
            bytes_accessed=12 * tokens_here * width,
            transcendentals=0,
        ),
        name="states",
    )(place, decay, drive, parts, totals, table, decay_gate, input_gate)


def products(c, gated, weights):
    deep = gated[0].shape[1]
    spots = [pl.multiple_of((c ^ e) * deep, deep) for e in range(2)]
    blocks = []
    for weight in weights:
        terms = [
            jnp.dot(
                gated[e][...], weight[pl.ds(spots[e], deep), :], preferred_element_type=jnp.float32
            )
            for e in range(2)
        ]
        blocks.append(terms[0] + terms[1])
    return blocks


def mix_near(place, parts, pieces):
    tokens_here, deep = parts[0].shape
    width = pieces[0].shape[1]
    rows = tokens_here // 2
    count = len(pieces)

    def kernel(place_ref, *refs):
        blocks = products(place_ref[0], refs[:2], refs[2:-1])
        for b in range(count):
            refs[-1][:, b * width : (b + 1) * width] = blocks[b]

    return pl.pallas_call(
        kernel,
        grid=(2,),
        out_shape=jax.ShapeDtypeStruct((tokens_here, count * width), jnp.float32),
        in_specs=[SMEM]
        + [pl.BlockSpec((rows, deep), lambda i: (i, 0))] * 2
        + [pl.BlockSpec(piece.shape, lambda i: (0, 0)) for piece in pieces],
        out_specs=pl.BlockSpec((rows, count * width), lambda i: (i, 0)),
        compiler_params=pltpu.CompilerParams(vmem_limit_bytes=GRANT),
        cost_estimate=pl.CostEstimate(
            flops=4 * count * tokens_here * deep * width,
            bytes_accessed=4 * tokens_here * deep + 8 * count * rows * width,
            transcendentals=0,
        ),
        name="mix_near",
    )(place, *parts, *pieces)


def mix_far(place, parts, pieces, near):
    tokens_here, deep = parts[0].shape
    width = pieces[0].shape[1]
    rows = tokens_here // 4
    count = len(pieces)
    parts = [value.reshape(2, 2, rows, deep) for value in parts]
    near = near.reshape(2, 2, rows, count * width)

    def kernel(place_ref, *refs):
        near_ref, leaves, stays = refs[-5], refs[-4:-2], refs[-2:]
        c = place_ref[0]
        gated = [ref[...].reshape(2 * rows, deep) for ref in refs[:2]]
        blocks = products(c, gated, refs[2:-5])
        sums = near_ref[...].reshape(2 * rows, count * width)
        blocks = [block + sums[:, b * width : (b + 1) * width] for b, block in enumerate(blocks)]

        def write(targets, order):
            for at_c in range(2):

                @pl.when(c == at_c)
                def write_runs():
                    for e, target in enumerate(targets):
                        run = at_c ^ e
                        for b in range(count):
                            at = order(b) * width
                            target[:, at : at + width] = blocks[b][
                                run * rows : (run + 1) * rows
                            ].astype(target.dtype)

        @pl.when(pl.program_id(0) == 0)
        def leave():
            write(leaves, lambda b: count - 1 - b)

        @pl.when(pl.program_id(0) == 1)
        def stay():
            write(stays, lambda b: b)

    def lows(f, p):
        return (0, 1 - f ^ p[6], 0, 0)

    grid_spec = pltpu.PrefetchScalarGridSpec(
        num_scalar_prefetch=1,
        grid=(2,),
        in_specs=[pl.BlockSpec((2, 1, rows, deep), lows) for _ in parts]
        + [pl.BlockSpec(piece.shape, lambda f, p: (0, 0)) for piece in pieces]
        + [pl.BlockSpec((2, 1, rows, count * width), lows)],
        out_specs=[pl.BlockSpec((rows, count * width), lambda f, p: (0, 0))] * 4,
    )
    kinds = [jnp.bfloat16, jnp.bfloat16, jnp.float32, jnp.bfloat16]
    return pl.pallas_call(
        kernel,
        grid_spec=grid_spec,
        out_shape=[jax.ShapeDtypeStruct((rows, count * width), kind) for kind in kinds],
        compiler_params=pltpu.CompilerParams(vmem_limit_bytes=GRANT),
        cost_estimate=pl.CostEstimate(
            flops=4 * count * tokens_here * deep * width,
            bytes_accessed=4 * tokens_here * deep + 28 * count * rows * width,
            transcendentals=0,
        ),
        name="mix_far",
    )(place, *parts, *pieces, near)


def place_columns(place, groups, terms, block):
    rows = terms[0].shape[0]
    segs = sum(len(group) for group in groups)

    def kernel(place_ref, *refs):
        c, z = place_ref[0], place_ref[1]
        whole = refs[-1]
        for i, group in enumerate(groups):
            for j, b in enumerate(group):
                for d in range(2):
                    at = pl.multiple_of(((c ^ d) * segs + (z ^ b)) * block, block)
                    one, two = (
                        ref[:, j * block : (j + 1) * block].astype(jnp.float32)
                        for ref in refs[4 * i + 2 * d : 4 * i + 2 * d + 2]
                    )
                    whole[:, pl.ds(at, block)] = (one + two).astype(whole.dtype)

    return pl.pallas_call(
        kernel,
        out_shape=jax.ShapeDtypeStruct((rows, 2 * segs * block), jnp.bfloat16),
        in_specs=[SMEM] + [VMEM] * len(terms),
        out_specs=VMEM,
        name="place",
    )(place, *terms)


def folded(
    tokens,
    x_weight,
    y_weight,
    out_weight,
    conv_weight,
    conv_bias,
    decay_gate,
    decay_bias,
    input_gate,
    input_bias,
    log_rate,
    phase,
):
    grps, segs = lax.axis_size("grp"), lax.axis_size("seg")
    g, z, y = lax.axis_index("grp"), lax.axis_index("seg"), lax.axis_index("mp")
    outer, highs = grps // 2, segs // 2
    x, c = g // 2, g % 2
    high, low = z // 2, z % 2
    turn = x ^ y
    rows, _ = tokens.shape
    columns = x_weight.shape[1]
    width = columns // 4
    taps = conv_weight.shape[0]
    length = 2 * rows
    place = jnp.stack([c, z, turn, x, low * 2 + c, high, low]).astype(jnp.int32)

    part = length // SUBS

    def less(count):
        c_all, s_all = jnp.cos(count * phase), jnp.sin(count * phase)
        c_few, s_few = jnp.cos((taps - 1) * phase), jnp.sin((taps - 1) * phase)
        return c_all * c_few + s_all * s_few, s_all * c_few - c_all * s_few

    table = jnp.stack(
        [conv_weight[k] for k in range(taps)]
        + [
            conv_bias,
            decay_bias,
            input_bias,
            -8.0 * jax.nn.softplus(log_rate),
            jnp.cos(phase),
            jnp.sin(phase),
            jnp.cos(part * phase),
            jnp.sin(part * phase),
            *less(length),
            *less(part),
        ]
    )

    by_z = swap(tokens, "seg", 1)
    here = [tokens, swap(tokens, "mp", 1), by_z, swap(by_z, "mp", 1)]
    tied, table = lax.optimization_barrier((tokens, table))
    there = [swap(piece, "grp", 1) for piece in [tied] + here[1:]]

    source = assemble(place, here + there, segs)

    def cut(weight, at_low, at_c):
        return lax.dynamic_slice(
            weight, (0, at_low * (2 * width) + at_c * width), (weight.shape[0], width)
        )

    def columns_of(weight):
        leaving = jnp.concatenate([cut(weight, low, 1 - c), cut(weight, 1 - low, 1 - c)])
        arrived = swap(leaving, "grp", 1)
        deep = weight.shape[0]
        own = jnp.concatenate([cut(weight, low, c), arrived[:deep]])
        other = jnp.concatenate([cut(weight, 1 - low, c), arrived[deep:]])
        return spread(own, other)

    x_near, x_far = columns_of(x_weight)
    y_near, y_far = columns_of(y_weight)

    half = 2 * width
    out_columns = out_weight.shape[1]
    out_near, out_far = spread(
        lax.dynamic_slice(out_weight, (low * half, 0), (half, out_columns)),
        lax.dynamic_slice(out_weight, ((1 - low) * half, 0), (half, out_columns)),
    )
    diagonal = turn == 0
    out_pieces = []
    for mine, theirs in zip(out_near, out_far):
        kept = jnp.where(diagonal, mine, theirs)
        passed = jnp.where(diagonal, theirs, mine)
        out_pieces.append((kept, swap(passed, "mp", 1)))

    (x_part,) = project(source, 0, x_near, last=False)
    (x_proj,) = project(source, 1, x_far, before=x_part)
    (y_part,) = project(source, 0, y_near, last=False)

    decay, drive, parts, total = run_gates(
        place, x_proj, table, decay_gate, input_gate, taps
    )
    totals = [total] + [swap(total, "seg", 2 * j) for j in range(1, highs)]
    totals = jnp.stack(totals)
    totals = [totals] + [swap(totals, "grp", 2 * i) for i in range(1, outer)]
    totals = jnp.stack(totals).reshape(outer * highs * 2, *total.shape[1:])
    state = run_states(
        place, decay, drive, parts, totals, table, decay_gate, input_gate, taps, outer, highs
    )

    (gated,) = project(source, 1, y_far, before=y_part, state=state)
    gated_y = swap(gated, "mp", 1)
    gated_near = [gated, swap(gated, "grp", 1)]
    gated_far = [gated_y, swap(gated_y, "grp", 1)]
    groups = [(b, b + 1) for b in range(0, segs - 2, 2)] + [(segs - 2,), (segs - 1,)]
    nears = []
    for group in groups:
        nears.append(mix_near(place, gated_near, [out_pieces[b][0] for b in group]))

    crossed = [
        (og * segs + oz, (og ^ 1) * segs + (oz ^ 1)) for og in range(grps) for oz in range(segs)
    ]
    kept, arrived = [], {}
    for group, near in zip(groups, nears):
        name = group[0]
        pieces = [out_pieces[b][1] for b in group]
        leave, leave_far, stay, stay_far = mix_far(place, gated_far, pieces, near)
        kept.append((stay, swap(stay_far, "grp", 1)))
        over = lax.ppermute(leave_far, ("grp", "seg"), crossed)
        partner = name if len(group) == 2 else name ^ 1
        arrived[partner] = (swap(leave, "seg", 1), over)
    terms = []
    for group, (stay, stay_far) in zip(groups, kept):
        leave, leave_far = arrived[group[0]]
        terms += [stay, leave, stay_far, leave_far]
    return place_columns(place, groups, terms, out_columns)


def solution(mesh):
    grps, segs, mps = mesh.shape["grp"], mesh.shape["seg"], mesh.shape["mp"]
    powers = segs >= 4 and segs & (segs - 1) == 0
    fits = grps == 2 * mps and mps == 2 and powers
    in_specs = (
        P(("grp", "seg"), "mp"),
        P(("grp", "seg"), "mp"),
        P(("grp", "seg"), "mp"),
        P("mp", ("grp", "seg")),
        P(None, "mp"),
        P("mp"),
        P("mp", None, None),
        P("mp"),
        P("mp", None, None),
        P("mp"),
        P("mp"),
        P("mp"),
    )
    out_specs = P(("grp", "seg"), "mp")

    def local(*arrays):
        return (folded if fits else general)(*arrays)

    return jax.shard_map(local, mesh=mesh, in_specs=in_specs, out_specs=out_specs, check_vma=False)
```
